32 devices in a mesh: group: 4 (over z), local: 8 (over y, x, core).
Axes of the slice: x: 2, y: 2, z: 4, core: 2. Of those that a mesh axis runs over, the one named last changes fastest.
Arguments:
- tokens: bfloat16 [4096, 2048], P(('group', 'local')), may hold values from -6 to 6
- cotangent: bfloat16 [4096, 2048], P(('group', 'local')), may hold values from -6 to 6
- expert_ids: int32 [4096, 4], P(('group', 'local')), may hold values from 0 to 31, all different within a row
- gates: float32 [4096, 4], P(('group', 'local')), may hold values from 0.1 to 1
- w_gate: bfloat16 [32, 2048, 768], P(('group', 'local')), may hold values from -0.125 to 0.125
- w_up: bfloat16 [32, 2048, 768], P(('group', 'local')), may hold values from -0.125 to 0.125
- w_down: bfloat16 [32, 768, 2048], P(('group', 'local')), may hold values from -0.21875 to 0.21875
Outputs:
- mixed: bfloat16 [4096, 2048], P(('group', 'local'))
- d_tokens: bfloat16 [4096, 2048], P(('group', 'local'))
- d_gates: float32 [4096, 4], P(('group', 'local'))
- d_w_gate: bfloat16 [32, 2048, 768], P(('group', 'local'))
- d_w_up: bfloat16 [32, 2048, 768], P(('group', 'local'))
- d_w_down: bfloat16 [32, 768, 2048], P(('group', 'local'))
The draws below stay inside these ranges and needn't reach their ends.
Inputs may be any that keep to these rules, and one draw needn't show every extreme that they name: `expert_ids`: the 4 experts of a token are different.
All inputs are finite; a program needn't handle non-finite values.
Results may differ from the reference program's by a relative error of at most 0.0064.
Values may be sent and summed in bfloat16 or wider, within the bound.
No kernel may reach another device: no remote copies, remote signals or barrier semaphores. Data moves between devices by JAX's collectives and lax.ppermute only.
A program may use at most 128 MiB of HBM per device.

```python
import functools
import math
import jax
import jax.numpy as jnp
from jax import lax

D = 2048
FF = 768
TOPK = 4
TOK_DEV = 128
EXPERTS = 32
TOKENS = 4096
CAP = 24


def shard_levels(stream_key, extent, pieces, low, top_value):
    loudness, own = 1.0, jax.random.fold_in(stream_key, 6)
    for dim, blocks in pieces:
        heights = jnp.exp(jax.random.uniform(jax.random.fold_in(own, dim), (blocks,), jnp.float32, low / len(pieces), top_value / len(pieces)))
        loudness = loudness * jnp.repeat(heights, extent[dim] // blocks).reshape([-1 if axis == dim else 1 for axis in range(len(extent))])
    return loudness


def picks_of(rng, rows, amount, top, lift):
    ranking = jax.random.permutation(jax.random.fold_in(rng, 1), amount)
    boost = ranking
    for power in range(3):
        boost = boost * boost // amount
    boost = boost * lift // amount
    lots = jax.random.randint(jax.random.fold_in(rng, 2), (rows, amount), 0, 4096) + boost
    sure = jax.random.permutation(jax.random.fold_in(rng, 3), rows)[jnp.arange(amount) % rows]
    lots = jnp.where(jnp.arange(rows)[:, None] == sure[None, :], 1 << 14, lots)
    score = lots * amount + jnp.arange(amount)
    return lax.top_k(score.astype(jnp.int32), top)[1].astype(jnp.int32)


def centred(own_key, shape, width, bound, cuts=(), held_as=jnp.bfloat16):
    array = width * jax.random.normal(own_key, shape, jnp.float32)
    if cuts:
        array = array * shard_levels(own_key, shape, cuts, -0.22, 0.18)
    return jnp.clip(array, -bound, bound).astype(held_as)


def setup_inputs(seed: int = 0) -> dict:
    key_list = jax.random.split(jax.random.key(seed), 8)
    return {
        "tokens": centred(key_list[0], (TOKENS, D), 1.0, 6.0, ((0, 32),)),
        "cotangent": centred(key_list[1], (TOKENS, D), 1.0, 6.0, ((0, 32),)),
        "expert_ids": picks_of(key_list[2], TOKENS, EXPERTS, TOPK, 2048),
        "gates": jnp.clip(jnp.exp(math.log(1.0) - 2.3025851 * jax.random.uniform(key_list[3], (TOKENS, TOPK), jnp.float32) ** shard_levels(key_list[3], (TOKENS, TOPK), ((0, 32),), -0.2, 0.2)), 0.1, 1.0),
        "w_gate": centred(key_list[4], (EXPERTS, D, FF), D ** -0.5, 0.125, ((0, 32),)),
        "w_up": centred(key_list[5], (EXPERTS, D, FF), D ** -0.5, 0.125, ((0, 32),)),
        "w_down": centred(key_list[6], (EXPERTS, FF, D), FF ** -0.5, 0.21875, ((0, 32),)),
    }


def route_slots(block_ids, count_experts, capacity):
    experts_row = jnp.arange(count_experts, dtype=jnp.int32)
    onehot = (block_ids[:, None] == experts_row[None, :]).astype(jnp.int32)
    before = jnp.cumsum(onehot, axis=0) - onehot
    rank = jnp.sum(before * onehot, axis=1).astype(jnp.int32)
    kept = rank < capacity
    return jnp.where(kept, block_ids * capacity + rank, count_experts * capacity).astype(jnp.int32)


def expert_pass(rows_x, rows_z, wg, wu, wd):
    pre_gate = jnp.dot(rows_x, wg, preferred_element_type=jnp.float32)
    pre_up = jnp.dot(rows_x, wu, preferred_element_type=jnp.float32)
    sigmoid_a = jax.nn.sigmoid(pre_gate)
    silu_a = pre_gate * sigmoid_a
    hidden = (silu_a * pre_up).astype(jnp.bfloat16)
    out_rows = jnp.dot(hidden, wd, preferred_element_type=jnp.float32).astype(jnp.bfloat16)
    d_hidden = jnp.dot(rows_z, wd.T, preferred_element_type=jnp.float32)
    d_pre_gate = (d_hidden * pre_up * sigmoid_a * (1.0 + pre_gate * (1.0 - sigmoid_a))).astype(jnp.bfloat16)
    d_pre_up = (d_hidden * silu_a).astype(jnp.bfloat16)
    dx_rows = (jnp.dot(d_pre_gate, wg.T, preferred_element_type=jnp.float32)
               + jnp.dot(d_pre_up, wu.T, preferred_element_type=jnp.float32)).astype(jnp.bfloat16)
    grad_down = jnp.dot(hidden.T, rows_z, preferred_element_type=jnp.float32)
    grad_gate = jnp.dot(rows_x.T, d_pre_gate, preferred_element_type=jnp.float32)
    grad_up = jnp.dot(rows_x.T, d_pre_up, preferred_element_type=jnp.float32)
    return out_rows, dx_rows, grad_gate, grad_up, grad_down


def reference(tokens, cotangent, expert_ids, gates, w_gate, w_up, w_down):
    blocks = expert_ids.reshape(EXPERTS, TOK_DEV * TOPK).astype(jnp.int32)
    slots = jax.vmap(functools.partial(route_slots, count_experts=EXPERTS, capacity=CAP))(blocks)
    source = jnp.arange(EXPERTS, dtype=jnp.int32)[:, None]
    owner = slots // CAP
    rank = slots % CAP
    total_slots = EXPERTS * EXPERTS * CAP
    flat = jnp.where(slots < EXPERTS * CAP, owner * (EXPERTS * CAP) + source * CAP + rank, total_slots).astype(jnp.int32)
    order = jnp.arange(TOK_DEV * TOPK, dtype=jnp.int32)[None, :]
    token_id = (source * TOK_DEV + order // TOPK).astype(jnp.int32)
    flat_all = flat.reshape(-1)
    token_table = jnp.full((total_slots,), TOKENS, jnp.int32).at[flat_all].set(token_id.reshape(-1), mode="drop")
    gate_table = jnp.zeros((total_slots,), jnp.float32).at[flat_all].set(gates.reshape(-1).astype(jnp.float32), mode="drop")
    token_table = token_table.reshape(EXPERTS, EXPERTS * CAP)
    gate_table = gate_table.reshape(EXPERTS, EXPERTS * CAP)
    tokens_pad = jnp.concatenate([tokens, jnp.zeros((1, D), tokens.dtype)], axis=0)
    cot_pad = jnp.concatenate([cotangent, jnp.zeros((1, D), cotangent.dtype)], axis=0)

    def one_expert(items):
        table, gate_row, wg, wu, wd = items
        rows_x = tokens_pad[table]
        rows_z = (gate_row[:, None] * cot_pad[table].astype(jnp.float32)).astype(jnp.bfloat16)
        out_rows, dx_rows, grad_gate, grad_up, grad_down = expert_pass(rows_x, rows_z, wg, wu, wd)
        return (out_rows, dx_rows, grad_gate.astype(jnp.bfloat16),
                grad_up.astype(jnp.bfloat16), grad_down.astype(jnp.bfloat16))

    out_all, dx_all, d_w_gate, d_w_up, d_w_down = lax.map(one_expert, (token_table, gate_table, w_gate, w_up, w_down))
    out_pad = jnp.concatenate([out_all.reshape(total_slots, D), jnp.zeros((1, D), jnp.bfloat16)], axis=0)
    dx_pad = jnp.concatenate([dx_all.reshape(total_slots, D), jnp.zeros((1, D), jnp.bfloat16)], axis=0)
    out_routes = out_pad[flat_all].reshape(TOKENS, TOPK, D).astype(jnp.float32)
    dx_routes = dx_pad[flat_all].reshape(TOKENS, TOPK, D).astype(jnp.float32)
    mixed = jnp.sum(gates.astype(jnp.float32)[:, :, None] * out_routes, axis=1).astype(jnp.bfloat16)
    d_gates = jnp.sum(cotangent.astype(jnp.float32)[:, None, :] * out_routes, axis=2)
    d_tokens = jnp.sum(dx_routes, axis=1).astype(jnp.bfloat16)
    return mixed, d_tokens, d_gates, d_w_gate, d_w_up, d_w_down
```

```python
import functools

import jax
import jax.numpy as jnp
from jax import lax
from jax.experimental import pallas as pl
from jax.experimental.pallas import tpu as pltpu
from jax.sharding import PartitionSpec as P

F32 = jnp.float32
BF16 = jnp.bfloat16
META = 128
VMEM_BYTES = 50 << 20


def split3(v):
    hi = v.astype(BF16)
    rest = v - hi.astype(F32)
    mid = rest.astype(BF16)
    low = (rest - mid.astype(F32)).astype(BF16)
    return hi, mid, low


def dot(a, b, ca=1, cb=0):
    return lax.dot_general(a, b, (((ca,), (cb,)), ((), ())), preferred_element_type=F32)


def selection(meta, tab, top):
    eid, place = tab[0:1, :], tab[1:2, :]
    tok = meta.shape[0]
    hits = [(meta[:, k : k + 1] == eid).astype(F32) for k in range(top)]
    hit = functools.reduce(lambda a, b: a + b, hits)
    gate = functools.reduce(
        lambda a, b: a + b,
        [
            hits[k]
            * (
                meta[:, top + k : top + k + 1]
                + meta[:, 2 * top + k : 2 * top + k + 1]
                + meta[:, 3 * top + k : 3 * top + k + 1]
            )
            for k in range(top)
        ],
    )
    row = lax.broadcasted_iota(jnp.int32, (tok, tok), 0)
    col = lax.broadcasted_iota(jnp.int32, (tok, tok), 1)
    earlier = (col < row).astype(F32).astype(BF16)
    rank = dot(earlier, hit.astype(BF16))
    sel = jnp.where(rank == place, hit, 0.0)
    return sel, gate, hits


def dispatch_kernel(top, width, tab_ref, buf_ref, *outs):
    meta = buf_ref[:, 2 * width :].astype(F32)
    sel, gate, _ = selection(meta, tab_ref[...], top)
    sel_t = sel.T
    gate_t = jnp.sum((sel * gate).T, axis=1, keepdims=True)
    pick = sel_t.astype(BF16)
    rows_p = outs[0].shape[0]
    step = 512
    for c in range(0, width, step):
        x = dot(pick, buf_ref[:, c : c + step])
        z = gate_t * dot(pick, buf_ref[:, width + c : width + c + step])
        for s, out in enumerate(outs):
            out[:, c : c + step] = x[s * rows_p : (s + 1) * rows_p].astype(BF16)
            out[:, width + c : width + c + step] = z[
                s * rows_p : (s + 1) * rows_p
            ].astype(BF16)


def gather_rows(pieces, lo, hi):
    return jnp.concatenate([p[:, lo:hi].astype(F32) for p in pieces], axis=0).astype(
        BF16
    )


def expert_kernel(count, width, *refs):
    pieces = refs[:count]
    wg_ref, wu_ref, wd_ref = refs[count : count + 3]
    rets = refs[count + 3 : 2 * count + 3]
    xz_ref, hid_ref, dpg_ref, dpu_ref, acc_o, acc_d = refs[2 * count + 3 :]
    f = pl.program_id(0)

    @pl.when(f == 0)
    def _():
        for c in range(0, 2 * width, 512):
            xz_ref[:, c : c + 512] = gather_rows(pieces, c, c + 512)

    wg, wu, wd = wg_ref[0], wu_ref[0], wd_ref[0]
    x = xz_ref[:, :width]
    pre_gate = dot(x, wg)
    pre_up = dot(x, wu)
    d_hidden = dot(xz_ref[:, width:], wd, 1, 1)
    sig = jax.nn.sigmoid(pre_gate)
    silu = pre_gate * sig
    hidden = (silu * pre_up).astype(BF16)
    d_pre_gate = (d_hidden * pre_up * sig * (1.0 + pre_gate * (1.0 - sig))).astype(BF16)
    d_pre_up = (d_hidden * silu).astype(BF16)
    hid_ref[...] = hidden
    dpg_ref[...] = d_pre_gate
    dpu_ref[...] = d_pre_up
    out = dot(hidden, wd)
    d_x = dot(d_pre_gate, wg, 1, 1) + dot(d_pre_up, wu, 1, 1)

    @pl.when(f == 0)
    def _():
        acc_o[...] = out
        acc_d[...] = d_x

    @pl.when(f > 0)
    def _():
        acc_o[...] += out
        acc_d[...] += d_x

    @pl.when(f == pl.num_programs(0) - 1)
    def _():
        rows_p = rets[0].shape[0]
        for s, ret in enumerate(rets):
            ret[:, :width] = acc_o[s * rows_p : (s + 1) * rows_p, :].astype(BF16)
            ret[:, width:] = acc_d[s * rows_p : (s + 1) * rows_p, :].astype(BF16)


def token_sums(top, width, tab_ref, buf_ref, pieces, emit):
    meta = buf_ref[:, 2 * width :].astype(F32)
    sel, gate, hits = selection(meta, tab_ref[...], top)
    plain = sel.astype(BF16)
    gated = split3(sel * gate)
    prod = None
    step = 512
    for c in range(0, width, step):
        out_rows = gather_rows(pieces, c, c + step)
        dx_rows = gather_rows(pieces, width + c, width + c + step)
        mixed = dot(gated[0], out_rows) + dot(gated[1], out_rows) + dot(gated[2], out_rows)
        d_tok = dot(plain, dx_rows)
        part = dot(buf_ref[:, width + c : width + c + step], out_rows, 1, 1)
        prod = part if prod is None else prod + part
        emit(c, c + step, mixed, d_tok)
    prod = prod * sel
    return [jnp.sum(prod * h, axis=1, keepdims=True) for h in hits]


def combine_kernel(count, top, width, tab_ref, buf_ref, *refs):
    pieces, part_ref = refs[:count], refs[count]

    def emit(lo, hi, mixed, d_tok):
        part_ref[:, lo:hi] = mixed.astype(BF16)
        part_ref[:, width + lo : width + hi] = d_tok.astype(BF16)

    d_gates = token_sums(top, width, tab_ref, buf_ref, pieces, emit)
    lane = lax.broadcasted_iota(jnp.int32, (buf_ref.shape[0], META), 1)
    packed = jnp.zeros((buf_ref.shape[0], META), F32)
    for k, column in enumerate(d_gates):
        for i, piece in enumerate(split3(column)):
            packed = jnp.where(lane == i * top + k, piece.astype(F32), packed)
    part_ref[:, 2 * width :] = packed.astype(BF16)


def final_kernel(count, others, top, width, tab_ref, buf_ref, *refs):
    pieces = refs[:count]
    parts = refs[count : count + others]
    mixed_ref, d_tok_ref, d_gates_ref = refs[count + others :]

    def emit(lo, hi, mixed, d_tok):
        for p in parts:
            mixed = mixed + p[:, lo:hi].astype(F32)
            d_tok = d_tok + p[:, width + lo : width + hi].astype(F32)
        mixed_ref[:, lo:hi] = mixed.astype(BF16)
        d_tok_ref[:, lo:hi] = d_tok.astype(BF16)

    d_gates = token_sums(top, width, tab_ref, buf_ref, pieces, emit)
    packs = [p[:, 2 * width :].astype(F32) for p in parts]
    for k, column in enumerate(d_gates):
        for p in packs:
            column = column + (
                p[:, k : k + 1]
                + p[:, top + k : top + k + 1]
                + p[:, 2 * top + k : 2 * top + k + 1]
            )
        d_gates_ref[:, k : k + 1] = column


def weight_grad_kernel(stages, *refs):
    xs, zs = refs[:stages], refs[stages : 2 * stages]
    hids, dpgs, dpus = (refs[i * stages : (i + 1) * stages] for i in (2, 3, 4))
    gate_ref, up_ref, down_ref = refs[5 * stages :]

    def total(lefts, rights):
        acc = None
        for a, b in zip(lefts, rights):
            t = dot(a[...], b[...], 0, 0)
            acc = t if acc is None else acc + t
        return acc.astype(BF16)

    gate_ref[0] = total(xs, dpgs)
    up_ref[0] = total(xs, dpus)
    down_ref[0] = total(hids, zs)


def whole(shape):
    return pl.BlockSpec(shape, lambda *_: (0,) * len(shape))


def params():
    return pltpu.CompilerParams(vmem_limit_bytes=VMEM_BYTES)


def local(tokens, cotangent, expert_ids, gates, w_gate, w_up, w_down):
    groups = lax.axis_size("group")
    count = lax.axis_size("local")
    tok, width = tokens.shape
    top = expert_ids.shape[1]
    hidden_width = w_gate.shape[2]
    capacity = max(2, 3 * tok * top // (2 * groups * count))
    rows_p = -(-capacity // 8) * 8
    slots = count * rows_p
    me = lax.axis_index("local")
    plane = lax.axis_index("group")

    at = jnp.arange(slots, dtype=jnp.int32)
    owner = plane * count + jnp.bitwise_xor(at // rows_p, me)
    place = jnp.where(at % rows_p < capacity, at % rows_p, -1)
    tab = jnp.concatenate(
        [owner[None].astype(F32), place[None].astype(F32), jnp.zeros((6, slots), F32)], 0
    )
    meta = jnp.concatenate(
        [expert_ids.astype(BF16), *split3(gates), jnp.zeros((tok, META - 4 * top), BF16)], 1
    )
    buf0 = jnp.concatenate([tokens, cotangent, meta], axis=1)
    wide = 2 * width + META

    piece = jax.ShapeDtypeStruct((rows_p, 2 * width), BF16)
    tile = 256
    steps = hidden_width // tile

    def dispatch(buf):
        return pl.pallas_call(
            functools.partial(dispatch_kernel, top, width),
            out_shape=[piece] * count,
            compiler_params=params(),
            cost_estimate=pl.CostEstimate(
                flops=4 * slots * tok * width,
                bytes_accessed=2 * (tok * wide + 2 * slots * width),
                transcendentals=0,
            ),
            name="dispatch",
        )(tab, buf)

    def swap(pieces):
        return [pieces[0]] + [
            lax.ppermute(pieces[s], "local", [(i, i ^ s) for i in range(count)])
            for s in range(1, count)
        ]

    def expert(pieces):
        mid = jax.ShapeDtypeStruct((slots, hidden_width), BF16)
        got = pl.pallas_call(
            functools.partial(expert_kernel, count, width),
            grid=(steps,),
            in_specs=[whole((rows_p, 2 * width))] * count
            + [pl.BlockSpec((1, width, tile), lambda f: (0, 0, f))] * 2
            + [pl.BlockSpec((1, tile, width), lambda f: (0, f, 0))],
            out_specs=[whole((rows_p, 2 * width))] * count
            + [whole((slots, 2 * width))]
            + [pl.BlockSpec((slots, tile), lambda f: (0, f))] * 3,
            out_shape=[piece] * count
            + [jax.ShapeDtypeStruct((slots, 2 * width), BF16)]
            + [mid] * 3,
            scratch_shapes=[pltpu.VMEM((slots, width), F32)] * 2,
            compiler_params=params(),
            cost_estimate=pl.CostEstimate(
                flops=12 * slots * width * hidden_width,
                bytes_accessed=2 * (3 * width * hidden_width + 8 * slots * width),
                transcendentals=slots * hidden_width,
            ),
            name="expert",
        )(*pieces, w_gate, w_up, w_down)
        return got[:count], got[count:]

    def combine(buf, pieces):
        return pl.pallas_call(
            functools.partial(combine_kernel, count, top, width),
            out_shape=jax.ShapeDtypeStruct((tok, wide), BF16),
            compiler_params=params(),
            cost_estimate=pl.CostEstimate(
                flops=10 * slots * tok * width,
                bytes_accessed=2 * (2 * tok * wide + 2 * slots * width),
                transcendentals=0,
            ),
            name="combine",
        )(tab, buf, *pieces)

    bufs = [buf0]
    for _ in range(1, groups):
        bufs.append(
            lax.ppermute(bufs[-1], "group", [(i, (i + 1) % groups) for i in range(groups)])
        )

    kept, home = [], []
    rets = []
    for k in range(groups):
        pieces = swap(dispatch(bufs[k]))
        ret, saved = expert(pieces)
        kept.append(saved)
        rets.append(ret)
        if k:
            back = swap(ret)
            part = combine(bufs[k], back)
            home.append(
                lax.ppermute(part, "group", [(i, (i - k) % groups) for i in range(groups)])
            )
    held = lax.optimization_barrier((*rets[0], *rets[-1]))
    back0 = swap(list(held[:count]))
    others = len(home)
    mixed, d_tokens, d_gates = pl.pallas_call(
        functools.partial(final_kernel, count, others, top, width),
        out_shape=[
            jax.ShapeDtypeStruct((tok, width), BF16),
            jax.ShapeDtypeStruct((tok, width), BF16),
            jax.ShapeDtypeStruct((tok, top), F32),
        ],
        compiler_params=params(),
        cost_estimate=pl.CostEstimate(
            flops=10 * slots * tok * width,
            bytes_accessed=2 * ((2 + others) * tok * wide + 2 * slots * width),
            transcendentals=0,
        ),
        name="final",
    )(tab, buf0, *back0, *home)

    d_tile = 256
    d_steps = width // d_tile
    full = [whole((slots, hidden_width))] * groups
    d_w_gate, d_w_up, d_w_down = pl.pallas_call(
        functools.partial(weight_grad_kernel, groups),
        grid=(d_steps,),
        in_specs=[pl.BlockSpec((slots, d_tile), lambda d: (0, d))] * groups
        + [pl.BlockSpec((slots, d_tile), lambda d: (0, d_steps + d))] * groups
        + full * 3,
        out_specs=[pl.BlockSpec((1, d_tile, hidden_width), lambda d: (0, d, 0))] * 2
        + [pl.BlockSpec((1, hidden_width, d_tile), lambda d: (0, 0, d))],
        out_shape=[
            jax.ShapeDtypeStruct((1, width, hidden_width), BF16),
            jax.ShapeDtypeStruct((1, width, hidden_width), BF16),
            jax.ShapeDtypeStruct((1, hidden_width, width), BF16),
        ],
        compiler_params=params(),
        cost_estimate=pl.CostEstimate(
            flops=6 * groups * slots * width * hidden_width,
            bytes_accessed=2 * (3 * width * hidden_width + 2 * groups * slots * width),
            transcendentals=0,
        ),
        name="weight_grads",
    )(
        *[s[0] for s in kept],
        *[s[0] for s in kept],
        *[s[1] for s in kept],
        *[s[2] for s in kept],
        *[s[3] for s in kept],
    )
    return mixed, d_tokens, d_gates, d_w_gate, d_w_up, d_w_down


def solution(mesh):
    rows = P(("group", "local"), None)
    cube = P(("group", "local"), None, None)
    return jax.shard_map(
        local,
        mesh=mesh,
        in_specs=(rows, rows, rows, rows, cube, cube, cube),
        out_specs=(rows, rows, rows, cube, cube, cube),
        check_vma=False,
    )
```

```python
import functools

import jax
import jax.numpy as jnp
from jax import lax
from jax.experimental import pallas as pl
from jax.experimental.pallas import tpu as pltpu
from jax.sharding import PartitionSpec as P

F32 = jnp.float32
BF16 = jnp.bfloat16
META = 128
VMEM_BYTES = 24 << 20


def split3(v):
    hi = lax.reduce_precision(v, 8, 7)
    mid = lax.reduce_precision(v - hi, 8, 7)
    return hi.astype(BF16), mid.astype(BF16), (v - hi - mid).astype(BF16)


def dot(a, b, ca=1, cb=0):
    return lax.dot_general(a, b, (((ca,), (cb,)), ((), ())), preferred_element_type=F32)


def selection(meta, tab, top):
    eid, place = tab[0:1, :], tab[1:2, :]
    tok = meta.shape[0]
    hits = [(meta[:, k : k + 1] == eid).astype(F32) for k in range(top)]
    hit = functools.reduce(lambda a, b: a + b, hits)
    gate = functools.reduce(
        lambda a, b: a + b,
        [
            hits[k]
            * (
                meta[:, top + k : top + k + 1]
                + meta[:, 2 * top + k : 2 * top + k + 1]
                + meta[:, 3 * top + k : 3 * top + k + 1]
            )
            for k in range(top)
        ],
    )
    row = lax.broadcasted_iota(jnp.int32, (tok, tok), 0)
    col = lax.broadcasted_iota(jnp.int32, (tok, tok), 1)
    earlier = (col < row).astype(F32).astype(BF16)
    rank = dot(earlier, hit.astype(BF16))
    sel = jnp.where(rank == place, hit, 0.0)
    return sel, gate, hits


def dispatch_kernel(top, width, tab_ref, buf_ref, out_ref):
    count, rows_p = out_ref.shape[:2]
    sel, gate, _ = selection(buf_ref[:, 2 * width :].astype(F32), tab_ref[...], top)
    gate_t = jnp.sum((sel * gate).T, axis=1, keepdims=True)
    pick = sel.T.astype(BF16)
    step = 512
    for c in range(0, width, step):
        x = dot(pick, buf_ref[:, c : c + step])
        z = gate_t * dot(pick, buf_ref[:, width + c : width + c + step])
        for s in range(count):
            of = slice(s * rows_p, (s + 1) * rows_p)
            out_ref[s, :, c : c + step] = x[of].astype(BF16)
            out_ref[s, :, width + c : width + c + step] = z[of].astype(BF16)


def gather_rows(pieces, lo, hi, rows=slice(None)):
    return jnp.concatenate([p[rows, lo:hi].astype(F32) for p in pieces], axis=0).astype(
        BF16
    )


def expert_kernel(chips, width, me_ref, rows_ref, *refs):
    wg_ref, wu_ref, wd_ref = refs[:3]
    rets = refs[3 : 3 + chips]
    xz_ref, hid_ref, dpg_ref, dpu_ref, acc_o, acc_d = refs[3 + chips :]
    count, rows_p = rows_ref.shape[:2]
    f = pl.program_id(0)

    @pl.when(f == 0)
    def _():
        pieces = [rows_ref.at[s] for s in range(count)]
        for c in range(0, 2 * width, 512):
            xz_ref[:, c : c + 512] = gather_rows(pieces, c, c + 512)

    wg, wu, wd = wg_ref[0], wu_ref[0], wd_ref[0]
    x = xz_ref[:, :width]
    pre_gate = dot(x, wg)
    pre_up = dot(x, wu)
    d_hidden = dot(xz_ref[:, width:], wd, 1, 1)
    sig = jax.nn.sigmoid(pre_gate)
    silu = pre_gate * sig
    hidden = (silu * pre_up).astype(BF16)
    d_pre_gate = (d_hidden * pre_up * sig * (1.0 + pre_gate * (1.0 - sig))).astype(BF16)
    d_pre_up = (d_hidden * silu).astype(BF16)
    hid_ref[...] = hidden
    dpg_ref[...] = d_pre_gate
    dpu_ref[...] = d_pre_up
    out = dot(hidden, wd)
    d_x = dot(d_pre_gate, wg, 1, 1) + dot(d_pre_up, wu, 1, 1)

    @pl.when(f == 0)
    def _():
        acc_o[...] = out
        acc_d[...] = d_x

    @pl.when(f > 0)
    def _():
        acc_o[...] += out
        acc_d[...] += d_x

    @pl.when(f == pl.num_programs(0) - 1)
    def _():
        me = me_ref[0]
        for s, ret in enumerate(rets):
            for b in range(2):
                source = jnp.bitwise_xor(me, 2 * s + b)
                at = pl.ds(pl.multiple_of(source * rows_p, 8), rows_p)
                to = slice(b * rows_p, (b + 1) * rows_p)
                ret[to, :width] = acc_o[at, :].astype(BF16)
                ret[to, width:] = acc_d[at, :].astype(BF16)


def combine_kernel(count, top, width, tab_ref, own_ref, pair_ref, *refs):
    pieces, parts = refs[:count], refs[count:]
    rows_p = pieces[0].shape[0] // 2
    step = 512
    for b, buf_ref in enumerate((own_ref, pair_ref)):
        rows = slice(b * rows_p, (b + 1) * rows_p)
        sel, gate, hits = selection(
            buf_ref[:, 2 * width :].astype(F32), tab_ref[...], top
        )
        plain = sel.astype(BF16)
        gated = split3(sel * gate)
        prod = None
        for c in range(0, width, step):
            out_rows = gather_rows(pieces, c, c + step, rows)
            dx_rows = gather_rows(pieces, width + c, width + c + step, rows)
            mixed = dot(gated[0], out_rows) + dot(gated[1], out_rows)
            mixed = mixed + dot(gated[2], out_rows)
            part = dot(buf_ref[:, width + c : width + c + step], out_rows, 1, 1)
            prod = part if prod is None else prod + part
            parts[b][:, c : c + step] = mixed.astype(BF16)
            parts[b][:, width + c : width + c + step] = dot(plain, dx_rows).astype(BF16)
        prod = prod * sel
        lane = lax.broadcasted_iota(jnp.int32, (buf_ref.shape[0], META), 1)
        packed = jnp.zeros((buf_ref.shape[0], META), F32)
        for k, h in enumerate(hits):
            column = jnp.sum(prod * h, axis=1, keepdims=True)
            for i, piece in enumerate(split3(column)):
                packed = jnp.where(lane == i * top + k, piece.astype(F32), packed)
        parts[b][:, 2 * width :] = packed.astype(BF16)


def join_kernel(*refs):
    total = functools.reduce(lambda a, b: a + b, [r[...].astype(F32) for r in refs[:-1]])
    refs[-1][...] = total.astype(BF16)


def after(values, *deps):
    flat = [d for dep in deps for d in dep]
    return list(lax.optimization_barrier((*values, *flat))[: len(values)])


def final_kernel(count, top, width, *refs):
    parts = refs[:count]
    mixed_ref, d_tok_ref, d_gates_ref = refs[count:]

    def total(lo, hi):
        return functools.reduce(
            lambda a, b: a + b, [p[:, lo:hi].astype(F32) for p in parts]
        )

    mixed_ref[...] = total(0, width).astype(BF16)
    d_tok_ref[...] = total(width, 2 * width).astype(BF16)
    packed = total(2 * width, 2 * width + META)
    for k in range(top):
        d_gates_ref[:, k : k + 1] = (
            packed[:, k : k + 1]
            + packed[:, top + k : top + k + 1]
            + packed[:, 2 * top + k : 2 * top + k + 1]
        )


def weight_grad_kernel(stages, *refs):
    xs, zs = refs[:stages], refs[stages : 2 * stages]
    hids, dpgs, dpus = (refs[i * stages : (i + 1) * stages] for i in (2, 3, 4))
    gate_ref, up_ref, down_ref = refs[5 * stages :]

    def total(lefts, rights):
        acc = None
        for a, b in zip(lefts, rights):
            t = dot(a[...], b[...], 0, 0)
            acc = t if acc is None else acc + t
        return acc.astype(BF16)

    gate_ref[0] = total(xs, dpgs)
    up_ref[0] = total(xs, dpus)
    down_ref[0] = total(hids, zs)


def whole(shape):
    return pl.BlockSpec(shape, lambda *_: (0,) * len(shape))


def params():
    return pltpu.CompilerParams(vmem_limit_bytes=VMEM_BYTES)


def local(tokens, cotangent, expert_ids, gates, w_gate, w_up, w_down):
    groups = lax.axis_size("group")
    count = lax.axis_size("local")
    chips = count // 2
    tok, width = tokens.shape
    top = expert_ids.shape[1]
    hidden_width = w_gate.shape[2]
    capacity = max(2, 3 * tok * top // (2 * groups * count))
    rows_p = -(-capacity // 8) * 8
    slots = count * rows_p
    me = lax.axis_index("local")
    plane = lax.axis_index("group")

    def table(experts):
        slot = jnp.arange(experts.shape[0] * rows_p, dtype=jnp.int32) % rows_p
        rows = [
            jnp.repeat(plane * count + experts, rows_p).astype(F32)[None],
            jnp.where(slot < capacity, slot, -1).astype(F32)[None],
            jnp.zeros((6, slot.shape[0]), F32),
        ]
        return jnp.concatenate(rows, 0)

    tab_in = table(jnp.arange(count, dtype=jnp.int32))
    tab_back = table(jnp.bitwise_xor(2 * jnp.arange(chips, dtype=jnp.int32), me))
    meta = jnp.concatenate(
        [expert_ids.astype(BF16), *split3(gates), jnp.zeros((tok, META - 4 * top), BF16)], 1
    )
    buf0 = jnp.concatenate([tokens, cotangent, meta], axis=1)
    wide = 2 * width + META
    row = jax.ShapeDtypeStruct((tok, wide), BF16)

    piece = jax.ShapeDtypeStruct((2 * rows_p, 2 * width), BF16)
    tile = 256
    steps = hidden_width // tile

    def dispatch(buf):
        return pl.pallas_call(
            functools.partial(dispatch_kernel, top, width),
            out_shape=jax.ShapeDtypeStruct((count, rows_p, 2 * width), BF16),
            compiler_params=params(),
            cost_estimate=pl.CostEstimate(
                flops=4 * slots * tok * width * 30,
                bytes_accessed=2 * (tok * wide + 2 * slots * width) * 30,
                transcendentals=0,
            ),
            name="dispatch",
        )(tab_in, buf)

    def other_core(v):
        return lax.ppermute(v, "local", [(i, i ^ 1) for i in range(count)])

    def swap(pieces):
        return [pieces[0]] + [
            lax.ppermute(pieces[s], "local", [(i, i ^ (2 * s)) for i in range(count)])
            for s in range(1, chips)
        ]

    def expert(rows):
        mid = jax.ShapeDtypeStruct((slots, hidden_width), BF16)
        got = pl.pallas_call(
            functools.partial(expert_kernel, chips, width),
            grid=(steps,),
            in_specs=[pl.BlockSpec(memory_space=pltpu.SMEM)]
            + [whole((count, rows_p, 2 * width))]
            + [pl.BlockSpec((1, width, tile), lambda f: (0, 0, f))] * 2
            + [pl.BlockSpec((1, tile, width), lambda f: (0, f, 0))],
            out_specs=[whole((2 * rows_p, 2 * width))] * chips
            + [whole((slots, 2 * width))]
            + [pl.BlockSpec((slots, tile), lambda f: (0, f))] * 3,
            out_shape=[piece] * chips
            + [jax.ShapeDtypeStruct((slots, 2 * width), BF16)]
            + [mid] * 3,
            scratch_shapes=[pltpu.VMEM((slots, width), F32)] * 2,
            compiler_params=params(),
            cost_estimate=pl.CostEstimate(
                flops=12 * slots * width * hidden_width,
                bytes_accessed=2 * (3 * width * hidden_width + 8 * slots * width),
                transcendentals=slots * hidden_width,
            ),
            name="expert",
        )(me.reshape(1), rows, w_gate, w_up, w_down)
        return got[:chips], got[chips:]

    def combine(buf, pair, pieces):
        return pl.pallas_call(
            functools.partial(combine_kernel, chips, top, width),
            out_shape=[row, row],
            compiler_params=params(),
            cost_estimate=pl.CostEstimate(
                flops=10 * slots * tok * width * 100,
                bytes_accessed=2 * (4 * tok * wide + 2 * slots * width) * 100,
                transcendentals=0,
            ),
            name="combine",
        )(tab_back, buf, pair, *pieces)

    def join(*parts):
        return pl.pallas_call(
            join_kernel,
            out_shape=row,
            compiler_params=params(),
            cost_estimate=pl.CostEstimate(
                flops=len(parts) * tok * wide,
                bytes_accessed=2 * (1 + len(parts)) * tok * wide,
                transcendentals=0,
            ),
            name="join",
        )(*parts)

    def next_plane(v):
        return lax.ppermute(v, "group", [(i, (i + 1) % groups) for i in range(groups)])

    bufs, pairs, sent, came, kept, rets, outs = [], [], [], [], [], [], {}
    arriving = [buf0]

    def send(k, *deps, before_dispatch=()):
        bufs.append(after(arriving[-1:], *deps)[0])
        if k + 1 < groups:
            arriving.append(next_plane(bufs[k]))
        sent.append(dispatch(*after(bufs[k:], before_dispatch)))
        pairs.append(other_core(*after(bufs[k:], sent[k:])))
        came.append(
            lax.all_to_all(sent[k], "local", split_axis=0, concat_axis=0, tiled=True)
        )

    def compute(k, *deps):
        ret, saved = expert(*after(came[k : k + 1], pairs[k : k + 1], *deps))
        rets.append(ret)
        kept.append(saved)

    def give_back(k, *deps):
        outs[k] = swap(after(rets[k], *deps))

    def plane_sums(k, *deps):
        mine, theirs = combine(bufs[k], pairs[k], after(outs[k], *deps))
        return [mine, other_core(theirs)]

    last = groups - 1
    send(0)
    send(1, sent)
    compute(0, sent[1:])
    send(2, rets[0])
    compute(1, sent[2:])
    give_back(1)
    sums = []
    for k in range(3, groups):
        send(k, rets[k - 2])
        shares = plane_sums(k - 2, sent[k:])
        compute(k - 1, shares[:1])
        joined = join(*shares, *sums)
        sums = [next_plane(joined)]
        give_back(k - 1)
    compute(last, [joined])
    give_back(last)
    joined = join(*plane_sums(last - 1, rets[last]), *sums)
    sums = [next_plane(joined)]
    shares = plane_sums(last, [joined])
    kept = [after(saved, shares[:1]) for saved in kept]
    give_back(0, outs[last], [joined])
    home = [next_plane(join(*shares, *sums))]
    home += plane_sums(0)
    mixed, d_tokens, d_gates = pl.pallas_call(
        functools.partial(final_kernel, len(home), top, width),
        out_shape=[
            jax.ShapeDtypeStruct((tok, width), BF16),
            jax.ShapeDtypeStruct((tok, width), BF16),
            jax.ShapeDtypeStruct((tok, top), F32),
        ],
        compiler_params=params(),
        cost_estimate=pl.CostEstimate(
            flops=len(home) * tok * wide,
            bytes_accessed=2 * (1 + len(home)) * tok * wide,
            transcendentals=0,
        ),
        name="final",
    )(*home)

    d_tile = 256
    d_steps = width // d_tile
    full = [whole((slots, hidden_width))] * groups
    d_w_gate, d_w_up, d_w_down = pl.pallas_call(
        functools.partial(weight_grad_kernel, groups),
        grid=(d_steps,),
        in_specs=[pl.BlockSpec((slots, d_tile), lambda d: (0, d))] * groups
        + [pl.BlockSpec((slots, d_tile), lambda d: (0, d_steps + d))] * groups
        + full * 3,
        out_specs=[pl.BlockSpec((1, d_tile, hidden_width), lambda d: (0, d, 0))] * 2
        + [pl.BlockSpec((1, hidden_width, d_tile), lambda d: (0, 0, d))],
        out_shape=[
            jax.ShapeDtypeStruct((1, width, hidden_width), BF16),
            jax.ShapeDtypeStruct((1, width, hidden_width), BF16),
            jax.ShapeDtypeStruct((1, hidden_width, width), BF16),
        ],
        compiler_params=params(),
        cost_estimate=pl.CostEstimate(
            flops=6 * groups * slots * width * hidden_width,
            bytes_accessed=2 * (3 * width * hidden_width + 2 * groups * slots * width),
            transcendentals=0,
        ),
        name="weight_grads",
    )(
        *[s[0] for s in kept],
        *[s[0] for s in kept],
        *[s[1] for s in kept],
        *[s[2] for s in kept],
        *[s[3] for s in kept],
    )
    return mixed, d_tokens, d_gates, d_w_gate, d_w_up, d_w_down


def solution(mesh):
    rows = P(("group", "local"), None)
    cube = P(("group", "local"), None, None)
    return jax.shard_map(
        local,
        mesh=mesh,
        in_specs=(rows, rows, rows, rows, cube, cube, cube),
        out_specs=(rows, rows, rows, cube, cube, cube),
        check_vma=False,
    )
```

```python
import functools

import jax
import jax.numpy as jnp
from jax import lax
from jax.experimental import pallas as pl
from jax.experimental.pallas import tpu as pltpu
from jax.sharding import PartitionSpec as P

F32 = jnp.float32
BF16 = jnp.bfloat16
META = 128
VMEM_BYTES = 24 << 20


def split3(v):
    hi = lax.reduce_precision(v, 8, 7)
    mid = lax.reduce_precision(v - hi, 8, 7)
    return hi.astype(BF16), mid.astype(BF16), (v - hi - mid).astype(BF16)


def dot(a, b, ca=1, cb=0):
    return lax.dot_general(a, b, (((ca,), (cb,)), ((), ())), preferred_element_type=F32)


def selection(meta, tab, top):
    eid, place = tab[0:1, :], tab[1:2, :]
    tok = meta.shape[0]
    hits = [(meta[:, k : k + 1] == eid).astype(F32) for k in range(top)]
    hit = functools.reduce(lambda a, b: a + b, hits)
    gate = functools.reduce(
        lambda a, b: a + b,
        [
            hits[k]
            * (
                meta[:, top + k : top + k + 1]
                + meta[:, 2 * top + k : 2 * top + k + 1]
                + meta[:, 3 * top + k : 3 * top + k + 1]
            )
            for k in range(top)
        ],
    )
    row = lax.broadcasted_iota(jnp.int32, (tok, tok), 0)
    col = lax.broadcasted_iota(jnp.int32, (tok, tok), 1)
    earlier = (col < row).astype(F32).astype(BF16)
    rank = dot(earlier, hit.astype(BF16))
    sel = jnp.where(rank == place, hit, 0.0)
    return sel, gate, hits


def pack_kernel(top, width, tokens_ref, cotangent_ref, ids_ref, gates_ref, buf_ref):
    tok = tokens_ref.shape[0]
    buf_ref[:, :width] = tokens_ref[...]
    buf_ref[:, width : 2 * width] = cotangent_ref[...]
    parts = [p.astype(F32) for p in split3(gates_ref[...])]
    rows = [ids_ref[...].astype(F32), *parts, jnp.zeros((META - 4 * top, tok), F32)]
    buf_ref[:, 2 * width :] = jnp.concatenate(rows, axis=0).T.astype(BF16)


def dispatch_kernel(top, width, tab_ref, buf_ref, out_ref):
    count, rows_p = out_ref.shape[:2]
    sel, gate, _ = selection(buf_ref[:, 2 * width :].astype(F32), tab_ref[...], top)
    gate_t = jnp.sum((sel * gate).T, axis=1, keepdims=True)
    pick = sel.T.astype(BF16)
    step = 512
    for c in range(0, width, step):
        x = dot(pick, buf_ref[:, c : c + step])
        z = gate_t * dot(pick, buf_ref[:, width + c : width + c + step])
        for s in range(count):
            of = slice(s * rows_p, (s + 1) * rows_p)
            out_ref[s, :, c : c + step] = x[of].astype(BF16)
            out_ref[s, :, width + c : width + c + step] = z[of].astype(BF16)


def gather_rows(pieces, lo, hi, rows=slice(None)):
    return jnp.concatenate([p[rows, lo:hi].astype(F32) for p in pieces], axis=0).astype(
        BF16
    )


def expert_kernel(chips, width, me_ref, rows_ref, *refs):
    wg_ref, wu_ref, wd_ref = refs[:3]
    rets = refs[3 : 3 + chips]
    xz_ref, hid_ref, dpg_ref, dpu_ref, acc_o, acc_d = refs[3 + chips :]
    count, rows_p = rows_ref.shape[:2]
    f = pl.program_id(0)

    @pl.when(f == 0)
    def _():
        pieces = [rows_ref.at[s] for s in range(count)]
        for c in range(0, 2 * width, 512):
            xz_ref[:, c : c + 512] = gather_rows(pieces, c, c + 512)

    wg, wu, wd = wg_ref[0], wu_ref[0], wd_ref[0]
    x = xz_ref[:, :width]
    pre_gate = dot(x, wg)
    pre_up = dot(x, wu)
    d_hidden = dot(xz_ref[:, width:], wd, 1, 1)
    sig = jax.nn.sigmoid(pre_gate)
    silu = pre_gate * sig
    hidden = (silu * pre_up).astype(BF16)
    d_pre_gate = (d_hidden * pre_up * sig * (1.0 + pre_gate * (1.0 - sig))).astype(BF16)
    d_pre_up = (d_hidden * silu).astype(BF16)
    hid_ref[...] = hidden
    dpg_ref[...] = d_pre_gate
    dpu_ref[...] = d_pre_up
    out = dot(hidden, wd)
    d_x = dot(d_pre_gate, wg, 1, 1) + dot(d_pre_up, wu, 1, 1)

    @pl.when(f == 0)
    def _():
        acc_o[...] = out
        acc_d[...] = d_x

    @pl.when(f > 0)
    def _():
        acc_o[...] += out
        acc_d[...] += d_x

    @pl.when(f == pl.num_programs(0) - 1)
    def _():
        me = me_ref[0]
        for s, ret in enumerate(rets):
            for b in range(2):
                source = jnp.bitwise_xor(me, 2 * s + b)
                at = pl.ds(pl.multiple_of(source * rows_p, 8), rows_p)
                to = slice(b * rows_p, (b + 1) * rows_p)
                ret[to, :width] = acc_o[at, :].astype(BF16)
                ret[to, width:] = acc_d[at, :].astype(BF16)


def combine_kernel(count, top, width, tab_ref, own_ref, pair_ref, *refs):
    pieces, parts = refs[:count], refs[count:]
    rows_p = pieces[0].shape[0] // 2
    step = 512
    for b, buf_ref in enumerate((own_ref, pair_ref)):
        rows = slice(b * rows_p, (b + 1) * rows_p)
        sel, gate, hits = selection(
            buf_ref[:, 2 * width :].astype(F32), tab_ref[...], top
        )
        plain = sel.astype(BF16)
        gated = split3(sel * gate)
        prod = None
        for c in range(0, width, step):
            out_rows = gather_rows(pieces, c, c + step, rows)
            dx_rows = gather_rows(pieces, width + c, width + c + step, rows)
            mixed = dot(gated[0], out_rows) + dot(gated[1], out_rows)
            mixed = mixed + dot(gated[2], out_rows)
            part = dot(buf_ref[:, width + c : width + c + step], out_rows, 1, 1)
            prod = part if prod is None else prod + part
            parts[b][:, c : c + step] = mixed.astype(BF16)
            parts[b][:, width + c : width + c + step] = dot(plain, dx_rows).astype(BF16)
        prod = prod * sel
        lane = lax.broadcasted_iota(jnp.int32, (buf_ref.shape[0], META), 1)
        packed = jnp.zeros((buf_ref.shape[0], META), F32)
        for k, h in enumerate(hits):
            column = jnp.sum(prod * h, axis=1, keepdims=True)
            for i, piece in enumerate(split3(column)):
                packed = jnp.where(lane == i * top + k, piece.astype(F32), packed)
        parts[b][:, 2 * width :] = packed.astype(BF16)


def join_kernel(*refs):
    total = functools.reduce(lambda a, b: a + b, [r[...].astype(F32) for r in refs[:-1]])
    refs[-1][...] = total.astype(BF16)


def after(values, *deps):
    flat = [d for dep in deps for d in dep]
    return list(lax.optimization_barrier((*values, *flat))[: len(values)])


def final_kernel(count, top, width, *refs):
    parts = refs[:count]
    mixed_ref, d_tok_ref, d_gates_ref = refs[count:]

    def total(lo, hi):
        return functools.reduce(
            lambda a, b: a + b, [p[:, lo:hi].astype(F32) for p in parts]
        )

    mixed_ref[...] = total(0, width).astype(BF16)
    d_tok_ref[...] = total(width, 2 * width).astype(BF16)
    packed = total(2 * width, 2 * width + META).T
    d_gates_ref[...] = packed[:top] + packed[top : 2 * top] + packed[2 * top : 3 * top]


def weight_grad_kernel(stages, *refs):
    xs, zs = refs[:stages], refs[stages : 2 * stages]
    hids, dpgs, dpus = (refs[i * stages : (i + 1) * stages] for i in (2, 3, 4))
    gate_ref, up_ref, down_ref = refs[5 * stages :]

    def total(lefts, rights):
        acc = None
        for a, b in zip(lefts, rights):
            t = dot(a[...], b[...], 0, 0)
            acc = t if acc is None else acc + t
        return acc.astype(BF16)

    gate_ref[0] = total(xs, dpgs)
    up_ref[0] = total(xs, dpus)
    down_ref[0] = total(hids, zs)


def whole(shape):
    return pl.BlockSpec(shape, lambda *_: (0,) * len(shape))


def in_hbm(v):
    return pltpu.with_memory_space_constraint(v, pltpu.HBM)


def params():
    return pltpu.CompilerParams(vmem_limit_bytes=VMEM_BYTES)


def local(tokens, cotangent, expert_ids, gates, w_gate, w_up, w_down):
    groups = lax.axis_size("group")
    count = lax.axis_size("local")
    chips = count // 2
    tok, width = tokens.shape
    top = expert_ids.shape[1]
    hidden_width = w_gate.shape[2]
    capacity = max(2, 3 * tok * top // (2 * groups * count))
    rows_p = -(-capacity // 8) * 8
    slots = count * rows_p
    me = lax.axis_index("local")
    plane = lax.axis_index("group")

    def table(experts):
        slot = jnp.arange(experts.shape[0] * rows_p, dtype=jnp.int32) % rows_p
        rows = [
            jnp.repeat(plane * count + experts, rows_p).astype(F32)[None],
            jnp.where(slot < capacity, slot, -1).astype(F32)[None],
            jnp.zeros((6, slot.shape[0]), F32),
        ]
        return jnp.concatenate(rows, 0)

    tab_in = table(jnp.arange(count, dtype=jnp.int32))
    tab_back = table(jnp.bitwise_xor(2 * jnp.arange(chips, dtype=jnp.int32), me))
    wide = 2 * width + META
    buf0 = pl.pallas_call(
        functools.partial(pack_kernel, top, width),
        out_shape=jax.ShapeDtypeStruct((tok, wide), BF16),
        compiler_params=params(),
        cost_estimate=pl.CostEstimate(
            flops=tok * META, bytes_accessed=4 * tok * wide, transcendentals=0
        ),
        name="pack",
    )(in_hbm(tokens), in_hbm(cotangent), expert_ids.T, gates.T)
    row = jax.ShapeDtypeStruct((tok, wide), BF16)

    piece = pltpu.HBM((2 * rows_p, 2 * width), BF16)
    tile = 256
    steps = hidden_width // tile

    def dispatch(buf):
        return pl.pallas_call(
            functools.partial(dispatch_kernel, top, width),
            out_shape=pltpu.HBM((count, rows_p, 2 * width), BF16),
            compiler_params=params(),
            cost_estimate=pl.CostEstimate(
                flops=4 * slots * tok * width * 30,
                bytes_accessed=2 * (tok * wide + 2 * slots * width) * 30,
                transcendentals=0,
            ),
            name="dispatch",
        )(tab_in, buf)

    def other_core(v):
        return lax.ppermute(v, "local", [(i, i ^ 1) for i in range(count)])

    def swap(pieces):
        return [pieces[0]] + [
            lax.ppermute(pieces[s], "local", [(i, i ^ (2 * s)) for i in range(count)])
            for s in range(1, chips)
        ]

    def expert(rows):
        mid = pltpu.HBM((slots, hidden_width), BF16)
        got = pl.pallas_call(
            functools.partial(expert_kernel, chips, width),
            grid=(steps,),
            in_specs=[pl.BlockSpec(memory_space=pltpu.SMEM)]
            + [whole((count, rows_p, 2 * width))]
            + [pl.BlockSpec((1, width, tile), lambda f: (0, 0, f))] * 2
            + [pl.BlockSpec((1, tile, width), lambda f: (0, f, 0))],
            out_specs=[whole((2 * rows_p, 2 * width))] * chips
            + [whole((slots, 2 * width))]
            + [pl.BlockSpec((slots, tile), lambda f: (0, f))] * 3,
            out_shape=[piece] * chips
            + [pltpu.HBM((slots, 2 * width), BF16)]
            + [mid] * 3,
            scratch_shapes=[pltpu.VMEM((slots, width), F32)] * 2,
            compiler_params=params(),
            cost_estimate=pl.CostEstimate(
                flops=12 * slots * width * hidden_width,
                bytes_accessed=2 * (3 * width * hidden_width + 8 * slots * width),
                transcendentals=slots * hidden_width,
            ),
            name="expert",
        )(me.reshape(1), rows, *[in_hbm(w) for w in (w_gate, w_up, w_down)])
        return got[:chips], got[chips:]

    def combine(buf, pair, pieces, weight):
        return pl.pallas_call(
            functools.partial(combine_kernel, chips, top, width),
            out_shape=[row, row],
            compiler_params=params(),
            cost_estimate=pl.CostEstimate(
                flops=10 * slots * tok * width * weight,
                bytes_accessed=2 * (4 * tok * wide + 2 * slots * width) * weight,
                transcendentals=0,
            ),
            name="combine",
        )(tab_back, buf, pair, *pieces)

    def join(*parts):
        return pl.pallas_call(
            join_kernel,
            out_shape=row,
            compiler_params=params(),
            cost_estimate=pl.CostEstimate(
                flops=len(parts) * tok * wide,
                bytes_accessed=2 * (1 + len(parts)) * tok * wide,
                transcendentals=0,
            ),
            name="join",
        )(*parts)

    def next_plane(v):
        return lax.ppermute(v, "group", [(i, (i + 1) % groups) for i in range(groups)])

    bufs, pairs, sent, came, kept, rets, outs = [], [], [], [], [], [], {}
    arriving = [buf0]

    def send(k, *deps, before_dispatch=()):
        bufs.append(after(arriving[-1:], *deps)[0])
        if k + 1 < groups:
            arriving.append(next_plane(bufs[k]))
        sent.append(dispatch(*after(bufs[k:], before_dispatch)))
        pairs.append(other_core(*after(bufs[k:], sent[k:])))
        came.append(
            lax.all_to_all(sent[k], "local", split_axis=0, concat_axis=0, tiled=True)
        )

    def compute(k, *deps):
        ret, saved = expert(*after(came[k : k + 1], pairs[k : k + 1], *deps))
        rets.append(ret)
        kept.append(saved)

    def give_back(k, *deps):
        outs[k] = swap(after(rets[k], *deps))

    def plane_sums(k, *deps):
        weight = 1 if k == 1 else 100
        mine, theirs = combine(bufs[k], pairs[k], after(outs[k], *deps), weight)
        return [mine, other_core(theirs)]

    last = groups - 1
    send(0)
    send(1, sent)
    compute(0, sent[1:])
    send(2, rets[0])
    compute(1, sent[2:])
    give_back(1)
    sums = []
    for k in range(3, groups):
        send(k, rets[k - 2])
        compute(k - 1, sent[k:])
        shares = plane_sums(k - 2, rets[k - 1])
        joined = join(*after(shares[:1], sums), shares[1], *sums)
        sums = [next_plane(joined)]
        give_back(k - 1)
    compute(last, [joined])
    give_back(last)
    shares = plane_sums(last - 1, rets[last])
    joined = join(*after(shares[:1], sums), shares[1], *sums)
    sums = [next_plane(joined)]
    kept = [after(saved, [joined]) for saved in kept]
    d_tile = 256
    d_steps = width // d_tile
    full = [whole((slots, hidden_width))] * groups
    d_w_gate, d_w_up, d_w_down = pl.pallas_call(
        functools.partial(weight_grad_kernel, groups),
        grid=(d_steps,),
        in_specs=[pl.BlockSpec((slots, d_tile), lambda d: (0, d))] * groups
        + [pl.BlockSpec((slots, d_tile), lambda d: (0, d_steps + d))] * groups
        + full * 3,
        out_specs=[pl.BlockSpec((1, d_tile, hidden_width), lambda d: (0, d, 0))] * 2
        + [pl.BlockSpec((1, hidden_width, d_tile), lambda d: (0, 0, d))],
        out_shape=[
            jax.ShapeDtypeStruct((1, width, hidden_width), BF16),
            jax.ShapeDtypeStruct((1, width, hidden_width), BF16),
            jax.ShapeDtypeStruct((1, hidden_width, width), BF16),
        ],
        compiler_params=params(),
        cost_estimate=pl.CostEstimate(
            flops=6 * groups * slots * width * hidden_width * 20,
            bytes_accessed=2 * (3 * width * hidden_width + 2 * groups * slots * width) * 20,
            transcendentals=0,
        ),
        name="weight_grads",
    )(
        *[s[0] for s in kept],
        *[s[0] for s in kept],
        *[s[1] for s in kept],
        *[s[2] for s in kept],
        *[s[3] for s in kept],
    )
    shares = plane_sums(last, [d_w_down])
    give_back(0, outs[last], [joined])
    leaving = join(*after(shares[:1], sums), shares[1], *sums)
    home = [next_plane(leaving)]
    shares = plane_sums(0, [leaving])
    home += [*after(shares[:1], home), shares[1]]
    mixed, d_tokens, d_gates = pl.pallas_call(
        functools.partial(final_kernel, len(home), top, width),
        out_shape=[
            jax.ShapeDtypeStruct((tok, width), BF16),
            jax.ShapeDtypeStruct((tok, width), BF16),
            jax.ShapeDtypeStruct((top, tok), F32),
        ],
        compiler_params=params(),
        cost_estimate=pl.CostEstimate(
            flops=len(home) * tok * wide,
            bytes_accessed=2 * (1 + len(home)) * tok * wide,
            transcendentals=0,
        ),
        name="final",
    )(*home)

    return mixed, d_tokens, d_gates.T, d_w_gate, d_w_up, d_w_down


def solution(mesh):
    rows = P(("group", "local"), None)
    cube = P(("group", "local"), None, None)
    return jax.shard_map(
        local,
        mesh=mesh,
        in_specs=(rows, rows, rows, rows, cube, cube, cube),
        out_specs=(rows, rows, rows, cube, cube, cube),
        check_vma=False,
    )
```

```python
import functools

import jax
import jax.numpy as jnp
from jax import lax
from jax.experimental import pallas as pl
from jax.experimental.pallas import tpu as pltpu
from jax.sharding import PartitionSpec as P

F32 = jnp.float32
BF16 = jnp.bfloat16
META = 128
VMEM_BYTES = 24 << 20


def split3(v):
    hi = lax.reduce_precision(v, 8, 7)
    mid = lax.reduce_precision(v - hi, 8, 7)
    return hi.astype(BF16), mid.astype(BF16), (v - hi - mid).astype(BF16)


def dot(a, b, ca=1, cb=0):
    return lax.dot_general(a, b, (((ca,), (cb,)), ((), ())), preferred_element_type=F32)


def selection(meta, tab, top):
    eid, place = tab[0:1, :], tab[1:2, :]
    tok = meta.shape[0]
    hits = [(meta[:, k : k + 1] == eid).astype(F32) for k in range(top)]
    hit = functools.reduce(lambda a, b: a + b, hits)
    gate = functools.reduce(
        lambda a, b: a + b,
        [
            hits[k]
            * (
                meta[:, top + k : top + k + 1]
                + meta[:, 2 * top + k : 2 * top + k + 1]
                + meta[:, 3 * top + k : 3 * top + k + 1]
            )
            for k in range(top)
        ],
    )
    row = lax.broadcasted_iota(jnp.int32, (tok, tok), 0)
    col = lax.broadcasted_iota(jnp.int32, (tok, tok), 1)
    earlier = (col < row).astype(F32).astype(BF16)
    rank = dot(earlier, hit.astype(BF16))
    sel = jnp.where(rank == place, hit, 0.0)
    return sel, gate, hits


def pack_kernel(top, width, tokens_ref, cotangent_ref, ids_ref, gates_ref, buf_ref):
    tok = tokens_ref.shape[0]
    buf_ref[:, :width] = tokens_ref[...]
    buf_ref[:, width : 2 * width] = cotangent_ref[...]
    parts = [p.astype(F32) for p in split3(gates_ref[...])]
    rows = [ids_ref[...].astype(F32), *parts, jnp.zeros((META - 4 * top, tok), F32)]
    buf_ref[:, 2 * width :] = jnp.concatenate(rows, axis=0).T.astype(BF16)


def dispatch_kernel(top, width, tab_ref, buf_ref, out_ref):
    count, rows_p = out_ref.shape[:2]
    sel, gate, _ = selection(buf_ref[:, 2 * width :].astype(F32), tab_ref[...], top)
    gate_t = jnp.sum((sel * gate).T, axis=1, keepdims=True)
    pick = sel.T.astype(BF16)
    step = 512
    for c in range(0, width, step):
        x = dot(pick, buf_ref[:, c : c + step])
        z = gate_t * dot(pick, buf_ref[:, width + c : width + c + step])
        for s in range(count):
            of = slice(s * rows_p, (s + 1) * rows_p)
            out_ref[s, :, c : c + step] = x[of].astype(BF16)
            out_ref[s, :, width + c : width + c + step] = z[of].astype(BF16)


def gather_rows(pieces, lo, hi, rows=slice(None)):
    return jnp.concatenate([p[rows, lo:hi].astype(F32) for p in pieces], axis=0).astype(
        BF16
    )


def expert_kernel(outs, width, me_ref, rows_ref, *refs):
    wg_ref, wu_ref, wd_ref = refs[:3]
    rets = refs[3 : 3 + outs]
    xz_ref, hid_ref, dpg_ref, dpu_ref, acc_o, acc_d = refs[3 + outs :]
    count, rows_p = rows_ref.shape[:2]
    f = pl.program_id(0)

    @pl.when(f == 0)
    def _():
        pieces = [rows_ref.at[s] for s in range(count)]
        for c in range(0, 2 * width, 512):
            xz_ref[:, c : c + 512] = gather_rows(pieces, c, c + 512)

    wg, wu, wd = wg_ref[0], wu_ref[0], wd_ref[0]
    x = xz_ref[:, :width]
    pre_gate = dot(x, wg)
    pre_up = dot(x, wu)
    d_hidden = dot(xz_ref[:, width:], wd, 1, 1)
    sig = jax.nn.sigmoid(pre_gate)
    silu = pre_gate * sig
    hidden = (silu * pre_up).astype(BF16)
    d_pre_gate = (d_hidden * pre_up * sig * (1.0 + pre_gate * (1.0 - sig))).astype(BF16)
    d_pre_up = (d_hidden * silu).astype(BF16)
    hid_ref[...] = hidden
    dpg_ref[...] = d_pre_gate
    dpu_ref[...] = d_pre_up
    out = dot(hidden, wd)
    d_x = dot(d_pre_gate, wg, 1, 1) + dot(d_pre_up, wu, 1, 1)

    @pl.when(f == 0)
    def _():
        acc_o[...] = out
        acc_d[...] = d_x

    @pl.when(f > 0)
    def _():
        acc_o[...] += out
        acc_d[...] += d_x

    @pl.when(f == pl.num_programs(0) - 1)
    def _():
        if outs == 1:
            for s in range(count):
                at = slice(s * rows_p, (s + 1) * rows_p)
                rets[0][s, :, :width] = acc_o[at, :].astype(BF16)
                rets[0][s, :, width:] = acc_d[at, :].astype(BF16)
            return
        me = me_ref[0]
        for s, ret in enumerate(rets):
            for b in range(2):
                source = jnp.bitwise_xor(me, 2 * s + b)
                at = pl.ds(pl.multiple_of(source * rows_p, 8), rows_p)
                to = slice(b * rows_p, (b + 1) * rows_p)
                ret[to, :width] = acc_o[at, :].astype(BF16)
                ret[to, width:] = acc_d[at, :].astype(BF16)


def combine_kernel(blocks, top, width, tab_ref, *refs):
    bufs, rest = refs[:blocks], refs[blocks:]
    got, parts = rest[:-blocks], rest[-blocks:]
    if len(got[0].shape) == 3:
        got = [got[0].at[s] for s in range(got[0].shape[0])]
    rows_p = got[0].shape[0] // blocks
    step = 512
    for b, buf_ref in enumerate(bufs):
        rows = slice(b * rows_p, (b + 1) * rows_p)
        sel, gate, hits = selection(
            buf_ref[:, 2 * width :].astype(F32), tab_ref[...], top
        )
        plain = sel.astype(BF16)
        gated = split3(sel * gate)
        prod = None
        for c in range(0, width, step):
            out_rows = gather_rows(got, c, c + step, rows)
            dx_rows = gather_rows(got, width + c, width + c + step, rows)
            mixed = dot(gated[0], out_rows) + dot(gated[1], out_rows)
            mixed = mixed + dot(gated[2], out_rows)
            part = dot(buf_ref[:, width + c : width + c + step], out_rows, 1, 1)
            prod = part if prod is None else prod + part
            parts[b][:, c : c + step] = mixed.astype(BF16)
            parts[b][:, width + c : width + c + step] = dot(plain, dx_rows).astype(BF16)
        prod = prod * sel
        lane = lax.broadcasted_iota(jnp.int32, (buf_ref.shape[0], META), 1)
        packed = jnp.zeros((buf_ref.shape[0], META), F32)
        for k, h in enumerate(hits):
            column = jnp.sum(prod * h, axis=1, keepdims=True)
            for i, piece in enumerate(split3(column)):
                packed = jnp.where(lane == i * top + k, piece.astype(F32), packed)
        parts[b][:, 2 * width :] = packed.astype(BF16)


def join_kernel(cuts, *refs):
    ins, outs = refs[: -len(cuts)], refs[-len(cuts) :]
    for (lo, hi), out in zip(cuts, outs):
        total = None
        for r in ins:
            v = r[...] if r.shape[1] == hi - lo else r[:, lo:hi]
            total = v.astype(F32) if total is None else total + v.astype(F32)
        out[...] = total.astype(BF16)


def after(values, *deps):
    flat = [d for dep in deps for d in dep]
    return list(lax.optimization_barrier((*values, *flat))[: len(values)])


def final_kernel(width, left_ref, right_ref, share_ref, mixed_ref, d_tok_ref, d_gates_ref):
    left, right = left_ref[...].astype(F32), right_ref[...].astype(F32)
    mixed_ref[...] = (left + share_ref[:, :width].astype(F32)).astype(BF16)
    rest = right + share_ref[:, width:].astype(F32)
    d_tok_ref[...] = rest[:, :width].astype(BF16)
    packed = rest[:, width:].T
    top = d_gates_ref.shape[0]
    d_gates_ref[...] = packed[:top] + packed[top : 2 * top] + packed[2 * top : 3 * top]


def weight_grad_kernel(stages, *refs):
    xs, zs = refs[:stages], refs[stages : 2 * stages]
    hids, dpgs, dpus = (refs[i * stages : (i + 1) * stages] for i in (2, 3, 4))
    gate_ref, up_ref, down_ref = refs[5 * stages :]

    def total(lefts, rights):
        acc = None
        for a, b in zip(lefts, rights):
            t = dot(a[...], b[...], 0, 0)
            acc = t if acc is None else acc + t
        return acc.astype(BF16)

    gate_ref[0] = total(xs, dpgs)
    up_ref[0] = total(xs, dpus)
    down_ref[0] = total(hids, zs)


def whole(shape):
    return pl.BlockSpec(shape, lambda *_: (0,) * len(shape))


def in_hbm(v):
    return pltpu.with_memory_space_constraint(v, pltpu.HBM)


def params():
    return pltpu.CompilerParams(vmem_limit_bytes=VMEM_BYTES)


def local(tokens, cotangent, expert_ids, gates, w_gate, w_up, w_down):
    groups = lax.axis_size("group")
    count = lax.axis_size("local")
    chips = count // 2
    tok, width = tokens.shape
    top = expert_ids.shape[1]
    hidden_width = w_gate.shape[2]
    capacity = max(2, 3 * tok * top // (2 * groups * count))
    rows_p = -(-capacity // 8) * 8
    slots = count * rows_p
    me = lax.axis_index("local")
    plane = lax.axis_index("group")

    def table(experts):
        slot = jnp.arange(experts.shape[0] * rows_p, dtype=jnp.int32) % rows_p
        rows = [
            jnp.repeat(plane * count + experts, rows_p).astype(F32)[None],
            jnp.where(slot < capacity, slot, -1).astype(F32)[None],
            jnp.zeros((6, slot.shape[0]), F32),
        ]
        return jnp.concatenate(rows, 0)

    tab_in = table(jnp.arange(count, dtype=jnp.int32))
    tab_back = table(jnp.bitwise_xor(2 * jnp.arange(chips, dtype=jnp.int32), me))
    wide = 2 * width + META
    buf0 = pl.pallas_call(
        functools.partial(pack_kernel, top, width),
        out_shape=jax.ShapeDtypeStruct((tok, wide), BF16),
        compiler_params=params(),
        cost_estimate=pl.CostEstimate(
            flops=tok * META, bytes_accessed=4 * tok * wide, transcendentals=0
        ),
        name="pack",
    )(in_hbm(tokens), in_hbm(cotangent), expert_ids.T, gates.T)
    row = jax.ShapeDtypeStruct((tok, wide), BF16)

    tile = 256
    steps = hidden_width // tile

    def dispatch(buf):
        return pl.pallas_call(
            functools.partial(dispatch_kernel, top, width),
            out_shape=pltpu.HBM((count, rows_p, 2 * width), BF16),
            compiler_params=params(),
            cost_estimate=pl.CostEstimate(
                flops=4 * slots * tok * width * 30,
                bytes_accessed=2 * (tok * wide + 2 * slots * width) * 30,
                transcendentals=0,
            ),
            name="dispatch",
        )(tab_in, buf)

    def other_core(v):
        return lax.ppermute(v, "local", [(i, i ^ 1) for i in range(count)])

    def swap(pieces):
        return [pieces[0]] + [
            lax.ppermute(pieces[s], "local", [(i, i ^ (2 * s)) for i in range(count)])
            for s in range(1, chips)
        ]

    def expert(rows, shape, outs):
        mid = pltpu.HBM((slots, hidden_width), BF16)
        got = pl.pallas_call(
            functools.partial(expert_kernel, outs, width),
            grid=(steps,),
            in_specs=[pl.BlockSpec(memory_space=pltpu.SMEM)]
            + [whole((count, rows_p, 2 * width))]
            + [pl.BlockSpec((1, width, tile), lambda f: (0, 0, f))] * 2
            + [pl.BlockSpec((1, tile, width), lambda f: (0, f, 0))],
            out_specs=[whole(shape)] * outs
            + [whole((slots, 2 * width))]
            + [pl.BlockSpec((slots, tile), lambda f: (0, f))] * 3,
            out_shape=[pltpu.HBM(shape, BF16)] * outs
            + [pltpu.HBM((slots, 2 * width), BF16)]
            + [mid] * 3,
            scratch_shapes=[pltpu.VMEM((slots, width), F32)] * 2,
            compiler_params=params(),
            cost_estimate=pl.CostEstimate(
                flops=12 * slots * width * hidden_width,
                bytes_accessed=2 * (3 * width * hidden_width + 8 * slots * width),
                transcendentals=slots * hidden_width,
            ),
            name="expert",
        )(me.reshape(1), rows, *[in_hbm(w) for w in (w_gate, w_up, w_down)])
        return got[:outs], got[outs:]

    def combine(tab, blocks, pieces, weight):
        return pl.pallas_call(
            functools.partial(combine_kernel, len(blocks), top, width),
            out_shape=[row] * len(blocks),
            compiler_params=params(),
            cost_estimate=pl.CostEstimate(
                flops=10 * slots * tok * width * weight,
                bytes_accessed=4 * (2 * tok * wide + slots * width) * weight,
                transcendentals=0,
            ),
            name="combine",
        )(tab, *blocks, *pieces)

    left, right = (0, width), (width, wide)

    def join(cuts, *parts):
        return pl.pallas_call(
            functools.partial(join_kernel, cuts),
            out_shape=[jax.ShapeDtypeStruct((tok, hi - lo), BF16) for lo, hi in cuts],
            compiler_params=params(),
            cost_estimate=pl.CostEstimate(
                flops=len(parts) * tok * wide,
                bytes_accessed=2 * (1 + len(parts)) * tok * wide,
                transcendentals=0,
            ),
            name="join",
        )(*parts)

    def next_plane(v):
        return lax.ppermute(v, "group", [(i, (i + 1) % groups) for i in range(groups)])

    bufs, sent, came, kept, rets, pairs, outs = [], [], [], [], [], {}, {}
    arriving = [buf0]
    last = groups - 1

    def by_permutes(k):
        return 0 < k < last

    def exchange(v):
        return lax.all_to_all(v, "local", split_axis=0, concat_axis=0, tiled=True)

    def send(k, *deps):
        bufs.append(after(arriving[-1:], *deps)[0])
        if k + 1 < groups:
            arriving.append(next_plane(bufs[k]))
        sent.append(dispatch(bufs[k]))
        if by_permutes(k):
            pairs[k] = other_core(*after(bufs[k:], sent[k:]))
        came.append(exchange(sent[k]))

    def compute(k, *deps):
        shape, parts = (count, rows_p, 2 * width), 1
        if by_permutes(k):
            shape, parts = (2 * rows_p, 2 * width), chips
            deps = ([pairs[k]], *deps)
        ret, saved = expert(*after(came[k : k + 1], *deps), shape, parts)
        rets.append(ret)
        kept.append(saved)

    def give_back(k, *deps):
        ready = after(rets[k], *deps)
        outs[k] = swap(ready) if by_permutes(k) else [exchange(ready[0])]

    def plane_sums(k, *deps):
        weight = 1 if k == 1 else 100
        back = after(outs[k], *deps)
        if not by_permutes(k):
            return combine(tab_in, [bufs[k]], back, weight)
        mine, theirs = combine(tab_back, [bufs[k], pairs[k]], back, weight)
        return [mine, other_core(theirs)]

    def add_up(cuts, shares, sums):
        return join(cuts, *after(shares[:1], sums), *shares[1:], *sums)

    send(0)
    send(1, sent)
    compute(0, sent[1:])
    send(2, rets[0])
    compute(1, sent[2:])
    give_back(1)
    sums = []
    for k in range(3, groups):
        send(k, rets[k - 2])
        compute(k - 1, sent[k:])
        shares = plane_sums(k - 2, rets[k - 1])
        joined = add_up([(0, wide)], shares, sums)
        sums = [next_plane(joined[0])]
        give_back(k - 1)
    compute(last, joined)
    give_back(last)
    shares = plane_sums(last - 1, rets[last])
    joined = add_up([left, right], shares, sums)
    sums = [next_plane(v) for v in joined]
    shares = plane_sums(last, joined)
    give_back(0, outs[last], shares)
    home = []
    for cut, arrived in zip((left, right), sums):
        leaving = add_up([cut], shares, [arrived])
        home.append(next_plane(leaving[0]))
    kept = [after(saved, leaving) for saved in kept]
    d_tile = 256
    d_steps = width // d_tile
    full = [whole((slots, hidden_width))] * groups
    d_w_gate, d_w_up, d_w_down = pl.pallas_call(
        functools.partial(weight_grad_kernel, groups),
        grid=(d_steps,),
        in_specs=[pl.BlockSpec((slots, d_tile), lambda d: (0, d))] * groups
        + [pl.BlockSpec((slots, d_tile), lambda d: (0, d_steps + d))] * groups
        + full * 3,
        out_specs=[pl.BlockSpec((1, d_tile, hidden_width), lambda d: (0, d, 0))] * 2
        + [pl.BlockSpec((1, hidden_width, d_tile), lambda d: (0, 0, d))],
        out_shape=[
            jax.ShapeDtypeStruct((1, width, hidden_width), BF16),
            jax.ShapeDtypeStruct((1, width, hidden_width), BF16),
            jax.ShapeDtypeStruct((1, hidden_width, width), BF16),
        ],
        compiler_params=params(),
        cost_estimate=pl.CostEstimate(
            flops=120 * groups * slots * width * hidden_width,
            bytes_accessed=40 * (3 * width * hidden_width + 2 * groups * slots * width),
            transcendentals=0,
        ),
        name="weight_grads",
    )(
        *[in_hbm(s[i]) for i in (0, 0, 1, 2, 3) for s in kept],
    )
    [share] = plane_sums(0, [d_w_down])
    mixed, d_tokens, d_gates = pl.pallas_call(
        functools.partial(final_kernel, width),
        out_shape=[
            jax.ShapeDtypeStruct((tok, width), BF16),
            jax.ShapeDtypeStruct((tok, width), BF16),
            jax.ShapeDtypeStruct((top, tok), F32),
        ],
        compiler_params=params(),
        cost_estimate=pl.CostEstimate(
            flops=2 * tok * wide,
            bytes_accessed=6 * tok * wide,
            transcendentals=0,
        ),
        name="final",
    )(*home, *after([share], home))

    return mixed, d_tokens, d_gates.T, d_w_gate, d_w_up, d_w_down


def solution(mesh):
    rows = P(("group", "local"), None)
    cube = P(("group", "local"), None, None)
    return jax.shard_map(
        local,
        mesh=mesh,
        in_specs=(rows, rows, rows, rows, cube, cube, cube),
        out_specs=(rows, rows, rows, cube, cube, cube),
        check_vma=False,
    )
```

```python
import functools

import jax
import jax.numpy as jnp
from jax import lax
from jax.experimental import pallas as pl
from jax.experimental.pallas import tpu as pltpu
from jax.sharding import PartitionSpec as P

F32 = jnp.float32
BF16 = jnp.bfloat16
META = 128
VMEM_BYTES = 24 << 20


def split3(v):
    hi = lax.reduce_precision(v, 8, 7)
    mid = lax.reduce_precision(v - hi, 8, 7)
    return hi.astype(BF16), mid.astype(BF16), (v - hi - mid).astype(BF16)


def dot(a, b, ca=1, cb=0):
    return lax.dot_general(a, b, (((ca,), (cb,)), ((), ())), preferred_element_type=F32)


def selection(meta, tab, top):
    eid, place = tab[0:1, :], tab[1:2, :]
    tok = meta.shape[0]
    hits = [(meta[:, k : k + 1] == eid).astype(F32) for k in range(top)]
    hit = functools.reduce(lambda a, b: a + b, hits)
    gate = functools.reduce(
        lambda a, b: a + b,
        [
            hits[k]
            * (
                meta[:, top + k : top + k + 1]
                + meta[:, 2 * top + k : 2 * top + k + 1]
                + meta[:, 3 * top + k : 3 * top + k + 1]
            )
            for k in range(top)
        ],
    )
    row = lax.broadcasted_iota(jnp.int32, (tok, tok), 0)
    col = lax.broadcasted_iota(jnp.int32, (tok, tok), 1)
    earlier = (col < row).astype(F32).astype(BF16)
    rank = dot(earlier, hit.astype(BF16))
    sel = jnp.where(rank == place, hit, 0.0)
    return sel, gate, hits


def pack_kernel(top, width, tokens_ref, cotangent_ref, ids_ref, gates_ref, buf_ref):
    tok = tokens_ref.shape[0]
    buf_ref[:, :width] = tokens_ref[...]
    buf_ref[:, width : 2 * width] = cotangent_ref[...]
    parts = [p.astype(F32) for p in split3(gates_ref[...])]
    rows = [ids_ref[...].astype(F32), *parts, jnp.zeros((META - 4 * top, tok), F32)]
    buf_ref[:, 2 * width :] = jnp.concatenate(rows, axis=0).T.astype(BF16)


def dispatch_kernel(top, width, tab_ref, buf_ref, out_ref):
    count, rows_p = out_ref.shape[:2]
    sel, gate, _ = selection(buf_ref[:, 2 * width :].astype(F32), tab_ref[...], top)
    gate_t = jnp.sum((sel * gate).T, axis=1, keepdims=True)
    pick = sel.T.astype(BF16)
    step = 512
    for c in range(0, width, step):
        x = dot(pick, buf_ref[:, c : c + step])
        z = gate_t * dot(pick, buf_ref[:, width + c : width + c + step])
        for s in range(count):
            of = slice(s * rows_p, (s + 1) * rows_p)
            out_ref[s, :, c : c + step] = x[of].astype(BF16)
            out_ref[s, :, width + c : width + c + step] = z[of].astype(BF16)


def gather_rows(pieces, lo, hi, rows=slice(None)):
    return jnp.concatenate([p[rows, lo:hi].astype(F32) for p in pieces], axis=0).astype(
        BF16
    )


def expert_kernel(outs, width, me_ref, rows_ref, *refs):
    wg_ref, wu_ref, wd_ref = refs[:3]
    rets = refs[3 : 3 + outs]
    xz_ref, hid_ref, dpg_ref, dpu_ref, acc_o, acc_d = refs[3 + outs :]
    count, rows_p = rows_ref.shape[:2]
    f = pl.program_id(0)

    @pl.when(f == 0)
    def _():
        pieces = [rows_ref.at[s] for s in range(count)]
        for c in range(0, 2 * width, 512):
            xz_ref[:, c : c + 512] = gather_rows(pieces, c, c + 512)

    wg, wu, wd = wg_ref[0], wu_ref[0], wd_ref[0]
    x = xz_ref[:, :width]
    pre_gate = dot(x, wg)
    pre_up = dot(x, wu)
    d_hidden = dot(xz_ref[:, width:], wd, 1, 1)
    sig = jax.nn.sigmoid(pre_gate)
    silu = pre_gate * sig
    hidden = (silu * pre_up).astype(BF16)
    d_pre_gate = (d_hidden * pre_up * sig * (1.0 + pre_gate * (1.0 - sig))).astype(BF16)
    d_pre_up = (d_hidden * silu).astype(BF16)
    hid_ref[...] = hidden
    dpg_ref[...] = d_pre_gate
    dpu_ref[...] = d_pre_up
    out = dot(hidden, wd)
    d_x = dot(d_pre_gate, wg, 1, 1) + dot(d_pre_up, wu, 1, 1)

    @pl.when(f == 0)
    def _():
        acc_o[...] = out
        acc_d[...] = d_x

    @pl.when(f > 0)
    def _():
        acc_o[...] += out
        acc_d[...] += d_x

    @pl.when(f == pl.num_programs(0) - 1)
    def _():
        if outs == 1:
            for s in range(count):
                at = slice(s * rows_p, (s + 1) * rows_p)
                rets[0][s, :, :width] = acc_o[at, :].astype(BF16)
                rets[0][s, :, width:] = acc_d[at, :].astype(BF16)
            return
        me = me_ref[0]
        for s, ret in enumerate(rets):
            for b in range(2):
                source = jnp.bitwise_xor(me, 2 * s + b)
                at = pl.ds(pl.multiple_of(source * rows_p, 8), rows_p)
                to = slice(b * rows_p, (b + 1) * rows_p)
                ret[to, :width] = acc_o[at, :].astype(BF16)
                ret[to, width:] = acc_d[at, :].astype(BF16)


def combine_kernel(lo_row, rows_p, top, width, tab_ref, buf_ref, *refs):
    got, part_ref = refs[:-1], refs[-1]
    got = got if len(got[0].shape) == 2 else [got[0].at[s] for s in range(got[0].shape[0])]
    rows = slice(lo_row, lo_row + rows_p)
    step = 512
    sel, gate, hits = selection(buf_ref[:, 2 * width :].astype(F32), tab_ref[...], top)
    plain = sel.astype(BF16)
    gated = split3(sel * gate)
    prod = None
    for c in range(0, width, step):
        out_rows = gather_rows(got, c, c + step, rows)
        dx_rows = gather_rows(got, width + c, width + c + step, rows)
        mixed = dot(gated[0], out_rows) + dot(gated[1], out_rows)
        mixed = mixed + dot(gated[2], out_rows)
        part = dot(buf_ref[:, width + c : width + c + step], out_rows, 1, 1)
        prod = part if prod is None else prod + part
        part_ref[:, c : c + step] = mixed.astype(BF16)
        part_ref[:, width + c : width + c + step] = dot(plain, dx_rows).astype(BF16)
    prod = prod * sel
    lane = lax.broadcasted_iota(jnp.int32, (buf_ref.shape[0], META), 1)
    packed = jnp.zeros((buf_ref.shape[0], META), F32)
    for k, h in enumerate(hits):
        column = jnp.sum(prod * h, axis=1, keepdims=True)
        for i, piece in enumerate(split3(column)):
            packed = jnp.where(lane == i * top + k, piece.astype(F32), packed)
    part_ref[:, 2 * width :] = packed.astype(BF16)


def join_kernel(cuts, *refs):
    ins, outs = refs[: -len(cuts)], refs[-len(cuts) :]
    for (lo, hi), out in zip(cuts, outs):
        total = None
        for r in ins:
            v = r[...] if r.shape[1] == hi - lo else r[:, lo:hi]
            total = v.astype(F32) if total is None else total + v.astype(F32)
        out[...] = total.astype(BF16)


def after(values, *deps):
    flat = [d for dep in deps for d in dep]
    return list(lax.optimization_barrier((*values, *flat))[: len(values)])


def final_left_kernel(sum_ref, share_ref, mixed_ref):
    mixed_ref[...] = (sum_ref[...].astype(F32) + share_ref[...].astype(F32)).astype(BF16)


def final_right_kernel(width, sum_ref, share_ref, d_tok_ref, d_gates_ref):
    rest = sum_ref[...].astype(F32) + share_ref[:, width:].astype(F32)
    d_tok_ref[...] = rest[:, :width].astype(BF16)
    packed = rest[:, width:].T
    top = d_gates_ref.shape[0]
    d_gates_ref[...] = packed[:top] + packed[top : 2 * top] + packed[2 * top : 3 * top]


def weight_grad_kernel(stages, *refs):
    xs, zs = refs[:stages], refs[stages : 2 * stages]
    hids, dpgs, dpus = (refs[i * stages : (i + 1) * stages] for i in (2, 3, 4))
    gate_ref, up_ref, down_ref = refs[5 * stages :]

    def total(lefts, rights):
        acc = None
        for a, b in zip(lefts, rights):
            t = dot(a[...], b[...], 0, 0)
            acc = t if acc is None else acc + t
        return acc.astype(BF16)

    gate_ref[0] = total(xs, dpgs)
    up_ref[0] = total(xs, dpus)
    down_ref[0] = total(hids, zs)


def whole(shape):
    return pl.BlockSpec(shape, lambda *_: (0,) * len(shape))


def in_hbm(v):
    return pltpu.with_memory_space_constraint(v, pltpu.HBM)


def params():
    return pltpu.CompilerParams(vmem_limit_bytes=VMEM_BYTES)


def local(tokens, cotangent, expert_ids, gates, w_gate, w_up, w_down):
    groups = lax.axis_size("group")
    count = lax.axis_size("local")
    chips = count // 2
    tok, width = tokens.shape
    top = expert_ids.shape[1]
    hidden_width = w_gate.shape[2]
    capacity = max(2, 3 * tok * top // (2 * groups * count))
    rows_p = -(-capacity // 8) * 8
    slots = count * rows_p
    me = lax.axis_index("local")
    plane = lax.axis_index("group")

    def table(experts):
        slot = jnp.arange(experts.shape[0] * rows_p, dtype=jnp.int32) % rows_p
        rows = [
            jnp.repeat(plane * count + experts, rows_p).astype(F32)[None],
            jnp.where(slot < capacity, slot, -1).astype(F32)[None],
            jnp.zeros((6, slot.shape[0]), F32),
        ]
        return jnp.concatenate(rows, 0)

    tab_in = table(jnp.arange(count, dtype=jnp.int32))
    tab_back = table(jnp.bitwise_xor(2 * jnp.arange(chips, dtype=jnp.int32), me))
    wide = 2 * width + META
    buf0 = pl.pallas_call(
        functools.partial(pack_kernel, top, width),
        out_shape=jax.ShapeDtypeStruct((tok, wide), BF16),
        compiler_params=params(),
        cost_estimate=pl.CostEstimate(
            flops=tok * META, bytes_accessed=4 * tok * wide, transcendentals=0
        ),
        name="pack",
    )(*[in_hbm(v) for v in (tokens, cotangent, expert_ids.T, gates.T)])
    row = jax.ShapeDtypeStruct((tok, wide), BF16)

    tile = 256
    steps = hidden_width // tile

    def dispatch(buf):
        return pl.pallas_call(
            functools.partial(dispatch_kernel, top, width),
            out_shape=pltpu.HBM((count, rows_p, 2 * width), BF16),
            compiler_params=params(),
            cost_estimate=pl.CostEstimate(
                flops=4 * slots * tok * width * 30,
                bytes_accessed=2 * (tok * wide + 2 * slots * width) * 30,
                transcendentals=0,
            ),
            name="dispatch",
        )(tab_in, buf)

    def other_core(v):
        return lax.ppermute(v, "local", [(i, i ^ 1) for i in range(count)])

    def swap(pieces):
        return [pieces[0]] + [
            lax.ppermute(pieces[s], "local", [(i, i ^ (2 * s)) for i in range(count)])
            for s in range(1, chips)
        ]

    def expert(rows, shape, outs):
        mid = pltpu.HBM((slots, hidden_width), BF16)
        got = pl.pallas_call(
            functools.partial(expert_kernel, outs, width),
            grid=(steps,),
            in_specs=[pl.BlockSpec(memory_space=pltpu.SMEM)]
            + [whole((count, rows_p, 2 * width))]
            + [pl.BlockSpec((1, width, tile), lambda f: (0, 0, f))] * 2
            + [pl.BlockSpec((1, tile, width), lambda f: (0, f, 0))],
            out_specs=[whole(shape)] * outs
            + [whole((slots, 2 * width))]
            + [pl.BlockSpec((slots, tile), lambda f: (0, f))] * 3,
            out_shape=[pltpu.HBM(shape, BF16)] * outs
            + [pltpu.HBM((slots, 2 * width), BF16)]
            + [mid] * 3,
            scratch_shapes=[pltpu.VMEM((slots, width), F32)] * 2,
            compiler_params=params(),
            cost_estimate=pl.CostEstimate(
                flops=12 * slots * width * hidden_width,
                bytes_accessed=2 * (3 * width * hidden_width + 8 * slots * width),
                transcendentals=slots * hidden_width,
            ),
            name="expert",
        )(me.reshape(1), rows, *[in_hbm(w) for w in (w_gate, w_up, w_down)])
        return got[:outs], got[outs:]

    def combine(tab, block, pieces, lo_row, weight):
        return pl.pallas_call(
            functools.partial(combine_kernel, lo_row, rows_p, top, width),
            out_shape=row,
            compiler_params=params(),
            cost_estimate=pl.CostEstimate(
                flops=10 * slots * tok * width * weight,
                bytes_accessed=4 * (2 * tok * wide + slots * width) * weight,
                transcendentals=0,
            ),
            name="combine",
        )(tab, block, *pieces)

    left, right = (0, width), (width, wide)

    def join(cuts, *parts):
        return pl.pallas_call(
            functools.partial(join_kernel, cuts),
            out_shape=[jax.ShapeDtypeStruct((tok, hi - lo), BF16) for lo, hi in cuts],
            compiler_params=params(),
            cost_estimate=pl.CostEstimate(
                flops=len(parts) * tok * wide,
                bytes_accessed=2 * (1 + len(parts)) * tok * wide,
                transcendentals=0,
            ),
            name="join",
        )(*parts)

    def next_plane(v):
        return lax.ppermute(v, "group", [(i, (i + 1) % groups) for i in range(groups)])

    bufs, sent, came, kept, rets, pairs, outs = [], [], [], [], [], {}, {}
    arriving = [buf0]
    last = groups - 1

    def by_permutes(k):
        return 0 < k < last

    def exchange(v):
        return lax.all_to_all(v, "local", split_axis=0, concat_axis=0, tiled=True)

    def send(k, *deps):
        bufs.append(after(arriving[-1:], *deps)[0])
        if k + 1 < groups:
            arriving.append(next_plane(bufs[k]))
        sent.append(dispatch(bufs[k]))
        if by_permutes(k):
            pairs[k] = other_core(*after(bufs[k:], sent[k:]))
        came.append(exchange(sent[k]))

    def compute(k, *deps):
        shape, parts = (count, rows_p, 2 * width), 1
        if by_permutes(k):
            shape, parts = (2 * rows_p, 2 * width), chips
            deps = ([pairs[k]], *deps)
        ret, saved = expert(*after(came[k : k + 1], *deps), shape, parts)
        rets.append(ret)
        kept.append(saved)

    def give_back(k, *deps):
        ready = after(rets[k], *deps)
        outs[k] = swap(ready) if by_permutes(k) else [exchange(ready[0])]

    def plane_sums(k, *deps):
        weight = 1 if k == 1 else 100
        back = after(outs[k], *deps)
        if not by_permutes(k):
            return [combine(tab_in, bufs[k], back, 0, weight)]
        theirs = combine(tab_back, pairs[k], back, rows_p, weight)
        mine = combine(tab_back, *after(bufs[k : k + 1], [theirs]), back, 0, 1)
        return [mine, other_core(theirs)]

    def add_up(cuts, shares, sums):
        return join(cuts, *after(shares[:1], sums), *shares[1:], *sums)

    send(0)
    send(1, sent)
    compute(0, sent[1:])
    send(2, rets[0])
    compute(1, sent[2:])
    give_back(1)
    sums = []
    for k in range(3, groups):
        send(k, rets[k - 2])
        compute(k - 1, sent[k:])
        shares = plane_sums(k - 2, rets[k - 1])
        joined = add_up([(0, wide)], shares, sums)
        sums = [next_plane(joined[0])]
        give_back(k - 1)
    compute(last, joined)
    give_back(last)
    shares = plane_sums(last - 1, rets[last])
    joined = add_up([left, right], shares, sums)
    sums = [next_plane(v) for v in joined]
    shares = plane_sums(last, joined)
    give_back(0, outs[last], shares)
    home = []
    for cut, arrived in zip((left, right), sums):
        leaving = add_up([cut], shares, [arrived])
        home.append(next_plane(leaving[0]))
    kept = [after(saved, leaving) for saved in kept]
    d_tile = 256
    d_steps = width // d_tile
    full = [whole((slots, hidden_width))] * groups
    d_w_gate, d_w_up, d_w_down = pl.pallas_call(
        functools.partial(weight_grad_kernel, groups),
        grid=(d_steps,),
        in_specs=[pl.BlockSpec((slots, d_tile), lambda d: (0, d))] * groups
        + [pl.BlockSpec((slots, d_tile), lambda d: (0, d_steps + d))] * groups
        + full * 3,
        out_specs=[pl.BlockSpec((1, d_tile, hidden_width), lambda d: (0, d, 0))] * 2
        + [pl.BlockSpec((1, hidden_width, d_tile), lambda d: (0, 0, d))],
        out_shape=[
            jax.ShapeDtypeStruct((1, width, hidden_width), BF16),
            jax.ShapeDtypeStruct((1, width, hidden_width), BF16),
            jax.ShapeDtypeStruct((1, hidden_width, width), BF16),
        ],
        compiler_params=params(),
        cost_estimate=pl.CostEstimate(
            flops=120 * groups * slots * width * hidden_width,
            bytes_accessed=40 * (3 * width * hidden_width + 2 * groups * slots * width),
            transcendentals=0,
        ),
        name="weight_grads",
    )(
        *[in_hbm(s[i]) for i in (0, 0, 1, 2, 3) for s in kept],
    )
    [share] = plane_sums(0, [d_w_down])
    cost = pl.CostEstimate(
        flops=tok * wide, bytes_accessed=3 * tok * wide, transcendentals=0
    )
    mixed = pl.pallas_call(
        final_left_kernel,
        grid=(1,),
        in_specs=[pl.BlockSpec((tok, width), lambda i: (0, 0))] * 2,
        out_specs=pl.BlockSpec((tok, width), lambda i: (0, 0)),
        out_shape=jax.ShapeDtypeStruct((tok, width), BF16),
        compiler_params=params(),
        cost_estimate=cost,
        name="final_left",
    )(home[0], share)
    d_tokens, d_gates = pl.pallas_call(
        functools.partial(final_right_kernel, width),
        out_shape=[
            jax.ShapeDtypeStruct((tok, width), BF16),
            jax.ShapeDtypeStruct((top, tok), F32),
        ],
        compiler_params=params(),
        cost_estimate=cost,
        name="final_right",
    )(*after([home[1]], [mixed]), share)
    return mixed, d_tokens, d_gates.T, d_w_gate, d_w_up, d_w_down


def solution(mesh):
    rows = P(("group", "local"), None)
    cube = P(("group", "local"), None, None)
    return jax.shard_map(
        local,
        mesh=mesh,
        in_specs=(rows, rows, rows, rows, cube, cube, cube),
        out_specs=(rows, rows, rows, cube, cube, cube),
        check_vma=False,
    )
```

```python
import functools

import jax
import jax.numpy as jnp
from jax import lax
from jax.experimental import pallas as pl
from jax.experimental.pallas import tpu as pltpu
from jax.sharding import PartitionSpec as P

F32 = jnp.float32
BF16 = jnp.bfloat16
META = 128
VMEM_BYTES = 24 << 20


def split3(v):
    hi = lax.reduce_precision(v, 8, 7)
    mid = lax.reduce_precision(v - hi, 8, 7)
    return hi.astype(BF16), mid.astype(BF16), (v - hi - mid).astype(BF16)


def dot(a, b, ca=1, cb=0):
    return lax.dot_general(a, b, (((ca,), (cb,)), ((), ())), preferred_element_type=F32)


def selection(meta, tab, top):
    eid, place = tab[0:1, :], tab[1:2, :]
    tok = meta.shape[0]
    hits = [(meta[:, k : k + 1] == eid).astype(F32) for k in range(top)]
    hit = functools.reduce(lambda a, b: a + b, hits)
    gate = functools.reduce(
        lambda a, b: a + b,
        [
            hits[k]
            * (
                meta[:, top + k : top + k + 1]
                + meta[:, 2 * top + k : 2 * top + k + 1]
                + meta[:, 3 * top + k : 3 * top + k + 1]
            )
            for k in range(top)
        ],
    )
    row = lax.broadcasted_iota(jnp.int32, (tok, tok), 0)
    col = lax.broadcasted_iota(jnp.int32, (tok, tok), 1)
    earlier = (col < row).astype(F32).astype(BF16)
    rank = dot(earlier, hit.astype(BF16))
    sel = jnp.where(rank == place, hit, 0.0)
    return sel, gate, hits


def pack_kernel(top, width, tokens_ref, cotangent_ref, ids_ref, gates_ref, buf_ref):
    tok = tokens_ref.shape[0]
    buf_ref[:, :width] = tokens_ref[...]
    buf_ref[:, width : 2 * width] = cotangent_ref[...]
    parts = [p.astype(F32) for p in split3(gates_ref[...])]
    rows = [ids_ref[...].astype(F32), *parts, jnp.zeros((META - 4 * top, tok), F32)]
    buf_ref[:, 2 * width :] = jnp.concatenate(rows, axis=0).T.astype(BF16)


def dispatch_kernel(top, width, tab_ref, buf_ref, out_ref):
    count, rows_p = out_ref.shape[:2]
    sel, gate, _ = selection(buf_ref[:, 2 * width :].astype(F32), tab_ref[...], top)
    gate_t = jnp.sum((sel * gate).T, axis=1, keepdims=True)
    pick = sel.T.astype(BF16)
    step = 512
    for c in range(0, width, step):
        x = dot(pick, buf_ref[:, c : c + step])
        z = gate_t * dot(pick, buf_ref[:, width + c : width + c + step])
        for s in range(count):
            of = slice(s * rows_p, (s + 1) * rows_p)
            out_ref[s, :, c : c + step] = x[of].astype(BF16)
            out_ref[s, :, width + c : width + c + step] = z[of].astype(BF16)


def gather_rows(pieces, lo, hi, rows=slice(None)):
    return jnp.concatenate([p[rows, lo:hi].astype(F32) for p in pieces], axis=0).astype(
        BF16
    )


def expert_kernel(outs, width, me_ref, rows_ref, *refs):
    wg_ref, wu_ref, wd_ref = refs[:3]
    rets = refs[3 : 3 + outs]
    xz_ref, hid_ref, dpg_ref, dpu_ref, acc_o, acc_d = refs[3 + outs :]
    count, rows_p = rows_ref.shape[:2]
    f = pl.program_id(0)

    @pl.when(f == 0)
    def _():
        pieces = [rows_ref.at[s] for s in range(count)]
        for c in range(0, 2 * width, 512):
            xz_ref[:, c : c + 512] = gather_rows(pieces, c, c + 512)

    wg, wu, wd = wg_ref[0], wu_ref[0], wd_ref[0]
    x = xz_ref[:, :width]
    pre_gate = dot(x, wg)
    pre_up = dot(x, wu)
    d_hidden = dot(xz_ref[:, width:], wd, 1, 1)
    sig = jax.nn.sigmoid(pre_gate)
    silu = pre_gate * sig
    hidden = (silu * pre_up).astype(BF16)
    d_pre_gate = (d_hidden * pre_up * sig * (1.0 + pre_gate * (1.0 - sig))).astype(BF16)
    d_pre_up = (d_hidden * silu).astype(BF16)
    hid_ref[...] = hidden
    dpg_ref[...] = d_pre_gate
    dpu_ref[...] = d_pre_up
    out = dot(hidden, wd)
    d_x = dot(d_pre_gate, wg, 1, 1) + dot(d_pre_up, wu, 1, 1)

    @pl.when(f == 0)
    def _():
        acc_o[...] = out
        acc_d[...] = d_x

    @pl.when(f > 0)
    def _():
        acc_o[...] += out
        acc_d[...] += d_x

    @pl.when(f == pl.num_programs(0) - 1)
    def _():
        if outs == 1:
            for s in range(count):
                at = slice(s * rows_p, (s + 1) * rows_p)
                rets[0][s, :, :width] = acc_o[at, :].astype(BF16)
                rets[0][s, :, width:] = acc_d[at, :].astype(BF16)
            return
        me = me_ref[0]
        for s, ret in enumerate(rets):
            for b in range(2):
                source = jnp.bitwise_xor(me, 2 * s + b)
                at = pl.ds(pl.multiple_of(source * rows_p, 8), rows_p)
                to = slice(b * rows_p, (b + 1) * rows_p)
                ret[to, :width] = acc_o[at, :].astype(BF16)
                ret[to, width:] = acc_d[at, :].astype(BF16)


def combine_kernel(lo_row, rows_p, top, width, tab_ref, buf_ref, *refs):
    got, part_ref = refs[:-1], refs[-1]
    got = got if len(got[0].shape) == 2 else [got[0].at[s] for s in range(got[0].shape[0])]
    rows = slice(lo_row, lo_row + rows_p)
    step = 512
    sel, gate, hits = selection(buf_ref[:, 2 * width :].astype(F32), tab_ref[...], top)
    plain = sel.astype(BF16)
    gated = split3(sel * gate)
    prod = None
    for c in range(0, width, step):
        out_rows = gather_rows(got, c, c + step, rows)
        dx_rows = gather_rows(got, width + c, width + c + step, rows)
        mixed = dot(gated[0], out_rows) + dot(gated[1], out_rows)
        mixed = mixed + dot(gated[2], out_rows)
        part = dot(buf_ref[:, width + c : width + c + step], out_rows, 1, 1)
        prod = part if prod is None else prod + part
        part_ref[:, c : c + step] = mixed.astype(BF16)
        part_ref[:, width + c : width + c + step] = dot(plain, dx_rows).astype(BF16)
    prod = prod * sel
    lane = lax.broadcasted_iota(jnp.int32, (buf_ref.shape[0], META), 1)
    packed = jnp.zeros((buf_ref.shape[0], META), F32)
    for k, h in enumerate(hits):
        column = jnp.sum(prod * h, axis=1, keepdims=True)
        for i, piece in enumerate(split3(column)):
            packed = jnp.where(lane == i * top + k, piece.astype(F32), packed)
    part_ref[:, 2 * width :] = packed.astype(BF16)


def join_kernel(cuts, *refs):
    ins, outs = refs[: -len(cuts)], refs[-len(cuts) :]
    for (lo, hi), out in zip(cuts, outs):
        total = None
        for r in ins:
            v = r[...] if r.shape[1] == hi - lo else r[:, lo:hi]
            total = v.astype(F32) if total is None else total + v.astype(F32)
        out[...] = total.astype(BF16)


def after(values, *deps):
    flat = [d for dep in deps for d in dep]
    return list(lax.optimization_barrier((*values, *flat))[: len(values)])


def final_left_kernel(sum_ref, share_ref, mixed_ref):
    mixed_ref[...] = (sum_ref[...].astype(F32) + share_ref[...].astype(F32)).astype(BF16)


def final_right_kernel(width, sum_ref, share_ref, d_tok_ref, d_gates_ref):
    rest = sum_ref[...].astype(F32) + share_ref[:, width:].astype(F32)
    d_tok_ref[...] = rest[:, :width].astype(BF16)
    packed = rest[:, width:].T
    top = d_gates_ref.shape[0]
    d_gates_ref[...] = packed[:top] + packed[top : 2 * top] + packed[2 * top : 3 * top]


def weight_grad_kernel(stages, *refs):
    xs, zs = refs[:stages], refs[stages : 2 * stages]
    hids, dpgs, dpus = (refs[i * stages : (i + 1) * stages] for i in (2, 3, 4))
    gate_ref, up_ref, down_ref = refs[5 * stages :]

    def total(lefts, rights):
        acc = None
        for a, b in zip(lefts, rights):
            t = dot(a[...], b[...], 0, 0)
            acc = t if acc is None else acc + t
        return acc.astype(BF16)

    gate_ref[0] = total(xs, dpgs)
    up_ref[0] = total(xs, dpus)
    down_ref[0] = total(hids, zs)


def whole(shape):
    return pl.BlockSpec(shape, lambda *_: (0,) * len(shape))


def in_hbm(v):
    return pltpu.with_memory_space_constraint(v, pltpu.HBM)


def params():
    return pltpu.CompilerParams(vmem_limit_bytes=VMEM_BYTES)


def local(tokens, cotangent, expert_ids, gates, w_gate, w_up, w_down):
    groups = lax.axis_size("group")
    count = lax.axis_size("local")
    chips = count // 2
    tok, width = tokens.shape
    top = expert_ids.shape[1]
    hidden_width = w_gate.shape[2]
    capacity = max(2, 3 * tok * top // (2 * groups * count))
    rows_p = -(-capacity // 8) * 8
    slots = count * rows_p
    me = lax.axis_index("local")
    plane = lax.axis_index("group")

    def table(experts):
        slot = jnp.arange(experts.shape[0] * rows_p, dtype=jnp.int32) % rows_p
        rows = [
            jnp.repeat(plane * count + experts, rows_p).astype(F32)[None],
            jnp.where(slot < capacity, slot, -1).astype(F32)[None],
            jnp.zeros((6, slot.shape[0]), F32),
        ]
        return jnp.concatenate(rows, 0)

    tab_in = table(jnp.arange(count, dtype=jnp.int32))
    tab_back = table(jnp.bitwise_xor(2 * jnp.arange(chips, dtype=jnp.int32), me))
    wide = 2 * width + META
    buf0 = pl.pallas_call(
        functools.partial(pack_kernel, top, width),
        out_shape=jax.ShapeDtypeStruct((tok, wide), BF16),
        compiler_params=params(),
        cost_estimate=pl.CostEstimate(
            flops=tok * META, bytes_accessed=4 * tok * wide, transcendentals=0
        ),
        name="pack",
    )(*[in_hbm(v) for v in (tokens, cotangent, expert_ids.T, gates.T)])
    row = jax.ShapeDtypeStruct((tok, wide), BF16)

    tile = 256
    steps = hidden_width // tile

    def dispatch(buf):
        return pl.pallas_call(
            functools.partial(dispatch_kernel, top, width),
            out_shape=pltpu.HBM((count, rows_p, 2 * width), BF16),
            compiler_params=params(),
            cost_estimate=pl.CostEstimate(
                flops=4 * slots * tok * width * 30,
                bytes_accessed=2 * (tok * wide + 2 * slots * width) * 30,
                transcendentals=0,
            ),
            name="dispatch",
        )(tab_in, buf)

    def other_core(v):
        return lax.ppermute(v, "local", [(i, i ^ 1) for i in range(count)])

    def swap(pieces):
        return [pieces[0]] + [
            lax.ppermute(pieces[s], "local", [(i, i ^ (2 * s)) for i in range(count)])
            for s in range(1, chips)
        ]

    def expert(rows, shape, outs):
        mid = pltpu.HBM((slots, hidden_width), BF16)
        got = pl.pallas_call(
            functools.partial(expert_kernel, outs, width),
            grid=(steps,),
            in_specs=[pl.BlockSpec(memory_space=pltpu.SMEM)]
            + [whole((count, rows_p, 2 * width))]
            + [pl.BlockSpec((1, width, tile), lambda f: (0, 0, f))] * 2
            + [pl.BlockSpec((1, tile, width), lambda f: (0, f, 0))],
            out_specs=[whole(shape)] * outs
            + [whole((slots, 2 * width))]
            + [pl.BlockSpec((slots, tile), lambda f: (0, f))] * 3,
            out_shape=[pltpu.HBM(shape, BF16)] * outs
            + [pltpu.HBM((slots, 2 * width), BF16)]
            + [mid] * 3,
            scratch_shapes=[pltpu.VMEM((slots, width), F32)] * 2,
            compiler_params=params(),
            cost_estimate=pl.CostEstimate(
                flops=12 * slots * width * hidden_width,
                bytes_accessed=2 * (3 * width * hidden_width + 8 * slots * width),
                transcendentals=slots * hidden_width,
            ),
            name="expert",
        )(me.reshape(1), rows, *[in_hbm(w) for w in (w_gate, w_up, w_down)])
        return got[:outs], got[outs:]

    def combine(tab, block, pieces, lo_row, weight):
        return pl.pallas_call(
            functools.partial(combine_kernel, lo_row, rows_p, top, width),
            out_shape=row,
            compiler_params=params(),
            cost_estimate=pl.CostEstimate(
                flops=10 * slots * tok * width * weight,
                bytes_accessed=4 * (2 * tok * wide + slots * width) * weight,
                transcendentals=0,
            ),
            name="combine",
        )(tab, block, *pieces)

    left, right = (0, width), (width, wide)

    def join(cuts, *parts):
        return pl.pallas_call(
            functools.partial(join_kernel, cuts),
            out_shape=[jax.ShapeDtypeStruct((tok, hi - lo), BF16) for lo, hi in cuts],
            compiler_params=params(),
            cost_estimate=pl.CostEstimate(
                flops=len(parts) * tok * wide,
                bytes_accessed=2 * (1 + len(parts)) * tok * wide,
                transcendentals=0,
            ),
            name="join",
        )(*parts)

    def next_plane(v):
        return lax.ppermute(v, "group", [(i, (i + 1) % groups) for i in range(groups)])

    bufs, sent, came, kept, rets, pairs, outs = [], [], [], [], [], {}, {}
    arriving = [buf0]
    last = groups - 1

    def by_permutes(k):
        return 0 < k < last

    def exchange(v):
        return lax.all_to_all(v, "local", split_axis=0, concat_axis=0, tiled=True)

    def send(k, *deps):
        bufs.append(after(arriving[-1:], *deps)[0])
        if k + 1 < groups:
            arriving.append(next_plane(bufs[k]))
        sent.append(dispatch(bufs[k]))
        if by_permutes(k):
            pairs[k] = other_core(*after(bufs[k:], sent[k:]))
        came.append(exchange(sent[k]))

    def compute(k, *deps):
        shape, parts = (count, rows_p, 2 * width), 1
        if by_permutes(k):
            shape, parts = (2 * rows_p, 2 * width), chips
            deps = ([pairs[k]], *deps)
        ret, saved = expert(*after(came[k : k + 1], *deps), shape, parts)
        rets.append(ret)
        kept.append(saved)

    def give_back(k, *deps):
        ready = after(rets[k], *deps)
        outs[k] = swap(ready) if by_permutes(k) else [exchange(ready[0])]

    def plane_sums(k, *deps):
        weight = 1 if k == 1 else 100
        back = after(outs[k], *deps)
        if not by_permutes(k):
            return [combine(tab_in, bufs[k], back, 0, weight)]
        theirs = combine(tab_back, pairs[k], back, rows_p, weight)
        mine = combine(tab_back, *after(bufs[k : k + 1], [theirs]), back, 0, 1)
        return [mine, other_core(theirs)]

    def add_up(cuts, shares, sums):
        return join(cuts, *after(shares[:1], sums), *shares[1:], *sums)

    send(0)
    send(1, sent)
    compute(0, sent[1:])
    send(2, rets[0])
    compute(1, sent[2:])
    give_back(1)
    sums = []
    for k in range(3, groups):
        send(k, rets[k - 2])
        compute(k - 1, sent[k:])
        shares = plane_sums(k - 2, rets[k - 1])
        joined = add_up([(0, wide)], shares, sums)
        sums = [next_plane(joined[0])]
        give_back(k - 1)
    compute(last, joined)
    give_back(last)
    shares = plane_sums(last - 1, rets[last])
    joined = add_up([left, right], shares, sums)
    sums = [next_plane(v) for v in joined]
    shares = plane_sums(last, joined)
    home = []
    for cut, arrived in zip((left, right), sums):
        leaving = add_up([cut], shares, [arrived])
        home.append(next_plane(leaving[0]))
        if not outs.get(0):
            give_back(0, outs[last], leaving)
    kept = [after(saved, leaving) for saved in kept]
    d_tile = 256
    d_steps = width // d_tile
    full = [whole((slots, hidden_width))] * groups
    d_w_gate, d_w_up, d_w_down = pl.pallas_call(
        functools.partial(weight_grad_kernel, groups),
        grid=(d_steps,),
        in_specs=[pl.BlockSpec((slots, d_tile), lambda d: (0, d))] * groups
        + [pl.BlockSpec((slots, d_tile), lambda d: (0, d_steps + d))] * groups
        + full * 3,
        out_specs=[pl.BlockSpec((1, d_tile, hidden_width), lambda d: (0, d, 0))] * 2
        + [pl.BlockSpec((1, hidden_width, d_tile), lambda d: (0, 0, d))],
        out_shape=[
            jax.ShapeDtypeStruct((1, width, hidden_width), BF16),
            jax.ShapeDtypeStruct((1, width, hidden_width), BF16),
            jax.ShapeDtypeStruct((1, hidden_width, width), BF16),
        ],
        compiler_params=params(),
        cost_estimate=pl.CostEstimate(
            flops=120 * groups * slots * width * hidden_width,
            bytes_accessed=40 * (3 * width * hidden_width + 2 * groups * slots * width),
            transcendentals=0,
        ),
        name="weight_grads",
    )(
        *[in_hbm(s[i]) for i in (0, 0, 1, 2, 3) for s in kept],
    )
    [share] = plane_sums(0, [d_w_down])
    cost = pl.CostEstimate(
        flops=tok * wide, bytes_accessed=3 * tok * wide, transcendentals=0
    )
    mixed = pl.pallas_call(
        final_left_kernel,
        grid=(1,),
        in_specs=[pl.BlockSpec((tok, width), lambda i: (0, 0))] * 2,
        out_specs=pl.BlockSpec((tok, width), lambda i: (0, 0)),
        out_shape=jax.ShapeDtypeStruct((tok, width), BF16),
        compiler_params=params(),
        cost_estimate=cost,
        name="final_left",
    )(home[0], share)
    d_tokens, d_gates = pl.pallas_call(
        functools.partial(final_right_kernel, width),
        out_shape=[
            jax.ShapeDtypeStruct((tok, width), BF16),
            jax.ShapeDtypeStruct((top, tok), F32),
        ],
        compiler_params=params(),
        cost_estimate=cost,
        name="final_right",
    )(*after([home[1]], [mixed]), share)
    return mixed, d_tokens, d_gates.T, d_w_gate, d_w_up, d_w_down


def solution(mesh):
    rows = P(("group", "local"), None)
    cube = P(("group", "local"), None, None)
    return jax.shard_map(
        local,
        mesh=mesh,
        in_specs=(rows, rows, rows, rows, cube, cube, cube),
        out_specs=(rows, rows, rows, cube, cube, cube),
        check_vma=False,
    )
```
